256 devices in a mesh: slab: 16 (over x, y_lo, core), blk: 16 (over z, y_hi).
Axes of the slice: x: 4, y: 4 (y_hi: 2, y_lo: 2; y = y_hi * 2 + y_lo), z: 8, core: 2. Of those that a mesh axis runs over, the one named last changes fastest.
Arguments:
- queries: bfloat16 [8192, 768], P(('slab', 'blk')), may hold values from -6 to 6
- passages: bfloat16 [8192, 768], P(('blk', 'slab')), may hold values from -6 to 6
- query_lognorm: float32 [8192], P(('slab', 'blk')), as said below
- passage_lognorm: float32 [8192], P('blk'), as said below
- loss_cotangent: float32 [], replicated, may hold values from 4 to 12
Outputs:
- query_gradient: float32 [8192, 768], P(('slab', 'blk'))
- passage_gradient: float32 [8192, 768], P(('blk', 'slab'))
The draws below stay inside these ranges and needn't reach their ends.
Inputs may be any that keep to these rules, and one draw needn't show every extreme that they name: `query_lognorm`: every entry lies between log(8192) + 0.5 and log(8192) + 3.5. `passage_lognorm`: every entry lies between log(8192) + 0.5 and log(8192) + 3.5.
All inputs are finite; a program needn't handle non-finite values.
Results may differ from the reference program's by a relative error of at most 0.034.
Values may be sent and summed in bfloat16 or wider, within the bound.
A program may use at most 64 MiB of HBM per device.

```python
import math
import jax
import jax.numpy as jnp
from jax import lax

D = 768
BATCH = 8192
N_SLAB = 16


def lognorm_values(key):
    offset = jnp.log(jnp.float32(BATCH))
    unit_draw = jax.random.uniform(key, (BATCH,), jnp.float32)
    return offset + 0.5 + 3.0 * unit_draw


def draw_query_lognorm(key, part):
    return lognorm_values(jax.random.fold_in(key, 11))


def draw_passage_lognorm(key, part):
    return lognorm_values(jax.random.fold_in(key, 23))


def shard_levels(rng, dims, split, smallest, top_value):
    def one(dim, blocks):
        draws = jax.random.uniform(jax.random.fold_in(jax.random.fold_in(rng, 6), dim), (blocks,), jnp.float32, smallest / len(split), top_value / len(split))
        return jnp.repeat(jnp.exp(draws), dims[dim] // blocks).reshape((-1,) + (1,) * (len(dims) - dim - 1))

    factor_of = one(*split[0])
    for cut in split[1:]:
        factor_of = factor_of * one(*cut)
    return factor_of


def scatter_about(stream_key, shape, scale, limit, cuts=(), kind=jnp.bfloat16):
    values = scale * jax.random.normal(stream_key, shape, jnp.float32)
    if cuts:
        values = values * shard_levels(stream_key, shape, cuts, -0.22, 0.18)
    return jnp.clip(values, -limit, limit).astype(kind)


def setup_inputs(seed: int = 0) -> dict:
    streams_of = jax.random.split(jax.random.key(seed), 6)
    queries = scatter_about(streams_of[0], (BATCH, D), 1.0, 6.0, ((0, 256),))
    passages = scatter_about(streams_of[1], (BATCH, D), 1.0, 6.0, ((0, 256),))
    query_lognorm = draw_query_lognorm(jax.random.fold_in(streams_of[5], 71), 0)
    passage_lognorm = draw_passage_lognorm(jax.random.fold_in(streams_of[5], 71), 0)
    loss_cotangent = jnp.clip(jax.random.uniform(streams_of[4], (), jnp.float32, 4.0, 12.0), 4.0, 12.0)
    return dict(queries=queries, passages=passages, query_lognorm=query_lognorm, passage_lognorm=passage_lognorm, loss_cotangent=loss_cotangent)


def reference(queries, passages, query_lognorm, passage_lognorm, loss_cotangent):
    score_scale = 2.0 / math.sqrt(D)
    half_cotangent = 0.5 * loss_cotangent
    query_blocks = queries.reshape(N_SLAB, BATCH // N_SLAB, D)
    norm_blocks = query_lognorm.reshape(N_SLAB, BATCH // N_SLAB)
    column_numbers = jnp.arange(BATCH, dtype=jnp.int32)
    block_numbers = jnp.arange(N_SLAB, dtype=jnp.int32)
    passages_wide = passages.astype(jnp.float32)

    def block_step(passage_total, inputs):
        query_rows, query_norms, block_index = inputs
        block_rows = query_rows.shape[0]
        scores = score_scale * lax.dot_general(query_rows, passages, (((1,), (1,)), ((), ())), preferred_element_type=jnp.float32)
        row_numbers = block_index * block_rows + jnp.arange(block_rows, dtype=jnp.int32)
        paired = (row_numbers[:, None] == column_numbers[None, :]).astype(jnp.float32)
        weights = half_cotangent * (jnp.exp(scores - query_norms[:, None]) + jnp.exp(scores - passage_lognorm[None, :]) - 2.0 * paired)
        rows_wide = query_rows.astype(jnp.float32)
        query_term = score_scale * jnp.dot(weights, passages_wide, precision=lax.Precision.HIGHEST, preferred_element_type=jnp.float32)
        passage_term = score_scale * lax.dot_general(weights, rows_wide, (((0,), (0,)), ((), ())), precision=lax.Precision.HIGHEST, preferred_element_type=jnp.float32)
        return (passage_total + passage_term, query_term)
    passage_total, query_terms = lax.scan(block_step, jnp.zeros((BATCH, D), jnp.float32), (query_blocks, norm_blocks, block_numbers))
    return (query_terms.reshape(BATCH, D), passage_total)
```

```python
import math

import jax
import jax.numpy as jnp
from jax import lax
from jax.experimental import pallas as pl
from jax.experimental.pallas import tpu as pltpu
from jax.sharding import PartitionSpec as P

MESH = pl.DeviceIdType.MESH
F32, BF16 = jnp.float32, jnp.bfloat16
ROWS = 32
HALF = 16
BATCH = 8192
LOG2E = math.log2(math.e)
TOP = math.log(BATCH) + 3.5
BOUND = 512 * 6.0 * 2.0**-30
TINY = 1e-37


def encode(value, inverse):
    t = value * inverse
    u = t * jnp.abs(t)
    return (u * jnp.abs(u)).astype(BF16)


def decode(coded, scale):
    wide = coded.astype(F32)
    r = lax.rsqrt(jnp.maximum(jnp.abs(wide), TINY))
    return (wide * r) * (r * lax.rsqrt(r)) * scale


def body(
    width,
    q_in, p_in, qn_in, pn_in, loss_ref,
    oq_ref, op_ref,
    q_all, p_all, qn_all, pn_all,
    w_hi, w_lo, g_q, g_p, xq_out, xq_in,
    zs1, zs2, zd_in, zf_in, zh_in, z2_in,
    pa_out, pa_in, pb_out, pb_in,
    fa_out, fa_in, fb_out, fb_in,
    sc_me, sc_q, sc_qr, sc_pa, sc_pb, sx_in, sz_in, sz2_in, sy1_in, sx1_in, sfa_in, sfb_in,
    ssem, lsem, q_sem, qh_sem, qn_sem, pa_sem, pb_sem, pn_sem,
    xq_sem, xs_sem, zd_sem, zf_sem, zh_sem, z2_sem, zsc_sem, zsc2_sem,
    ra_sem, rb_sem, ras_sem, rbs_sem, fa_sem, fb_sem, fas_sem, fbs_sem,
):
    slab, blk = lax.axis_index("slab"), lax.axis_index("blk")
    x, yl, c = slab // 4, (slab // 2) % 2, slab % 2
    z, yh = blk // 2, blk % 2
    y = yh * 2 + yl
    other = 1 - c
    same = c == yh

    def dev(xx, yy, zz, cc):
        return (xx * 4 + (yy % 2) * 2 + cc, zz * 2 + yy // 2)

    def up(value, by, size):
        return (value + by) % size

    pending = []
    count = [0]

    def send(build, when=None):
        index = count[0]
        count[0] += 1

        def make():
            src, dst, rsem, to = build()
            return pltpu.make_async_remote_copy(
                src_ref=src, dst_ref=dst, send_sem=ssem.at[index], recv_sem=rsem, device_id=to, device_id_type=MESH
            )

        if when is None:
            make().start()
        else:
            pl.when(when)(lambda: make().start())
        pending.append((make, when))

    def wait(dst, rsem):
        pltpu.make_async_remote_copy(
            src_ref=dst, dst_ref=dst, send_sem=lsem.at[0], recv_sem=rsem, device_id=dev(x, y, z, other), device_id_type=MESH
        ).wait_recv()

    barrier = pltpu.get_barrier_semaphore()
    peers = [dev(x, y, z, other)]
    peers += [dev(x, y, up(z, d, 8), c) for d in (1, 2, 6, 7)]
    peers += [dev(up(x, d, 4), y, z, cc) for d in (1, 2, 3) for cc in (0, 1)]
    peers += [dev(x, up(y, d, 4), z, cc) for d in (1, 2, 3) for cc in (0, 1)]
    for peer in peers:
        pl.semaphore_signal(barrier, inc=1, device_id=peer, device_id_type=MESH)

    me_q = c * 8 + z
    local_q = pltpu.make_async_copy(q_in, q_all.at[me_q], lsem.at[1])
    local_q.start()
    qn_all[me_q, :, :ROWS] = qn_in[...].reshape(1, ROWS)
    low, high = pl.ds(0, HALF), pl.ds(HALF, HALF)

    def local_p(half, sem):
        return pltpu.make_async_copy(p_in.at[half], p_all.at[slab, half], sem.at[slab])

    def local_pn():
        return pltpu.make_async_copy(pn_in, pn_all.at[0], pn_sem.at[0])

    @pl.when(same)
    def _():
        local_p(low, pa_sem).start()
        local_p(high, pb_sem).start()
        local_pn().start()

    pl.semaphore_wait(barrier, len(peers))

    for d in (2, 1, 3):
        send(lambda d=d: (p_in.at[low], p_all.at[slab, low], pa_sem.at[slab], dev(up(x, d, 4), y, z, yh)))
        send(lambda d=d: (p_in.at[high], p_all.at[slab, high], pb_sem.at[slab], dev(x, up(y, d, 4), z, yh)))
    for d in (2, 6, 1, 7):
        send(lambda d=d: (q_in, q_all.at[me_q], q_sem.at[me_q], dev(x, y, up(z, d, 8), c)))
        send(lambda d=d: (qn_all.at[me_q], qn_all.at[me_q], qn_sem.at[me_q], dev(x, y, up(z, d, 8), c)))
    send(lambda: (p_in.at[low], p_all.at[slab, low], pa_sem.at[slab], dev(x, y, z, other)), jnp.logical_not(same))
    send(lambda: (p_in.at[high], p_all.at[slab, high], pb_sem.at[slab], dev(x, y, z, other)), jnp.logical_not(same))
    send(lambda: (pn_in, pn_all.at[0], pn_sem.at[0], dev(x, up(y, 2, 4), z, c)), same)

    def q_send(slot, to, half=None, sem=None, norm=True):
        if half is None:
            send(lambda: (q_all.at[slot], q_all.at[slot], q_sem.at[slot], to))
        else:
            send(lambda: (q_all.at[slot, half], q_all.at[slot, half], sem, to))
        if norm:
            row = lambda: qn_all.at[slot]
            send(lambda: (row(), row(), qn_sem.at[slot], to))

    def q_wait(slot, norm=True):
        wait(q_all.at[slot], q_sem.at[slot])
        if norm:
            wait(qn_all.at[slot], qn_sem.at[slot])

    partner = dev(x, y, z, other)
    send(lambda: (q_in, q_all.at[me_q], q_sem.at[me_q], partner))
    send(lambda: (qn_all.at[me_q], qn_all.at[me_q], qn_sem.at[me_q], partner))

    for d, near, far, half, hsem in ((6, 1, 2, low, 0), (2, 7, 6, high, 1)):
        slot = c * 8 + up(z, d, 8)
        q_wait(slot)
        q_send(slot, dev(x, y, up(z, far, 8), c), half, qh_sem.at[hsem], norm=hsem == 0)
        q_send(slot, dev(x, y, up(z, near, 8), c))
        q_send(slot, partner)
    for d in (1, 7):
        slot = c * 8 + up(z, d, 8)
        q_wait(slot)
        q_send(slot, partner)

    for e in (0, 1, 3, 2):
        for cc in (0, 1):
            slot = up(x, e, 4) * 4 + yl * 2 + cc
            pl.when(same)(lambda slot=slot: wait(p_all.at[slot, low], pa_sem.at[slot]))
            for d in (2, 1, 3):
                send(
                    lambda slot=slot, d=d: (
                        p_all.at[slot, low], p_all.at[slot, low], pa_sem.at[slot], dev(x, up(y, d, 4), z, c)
                    ),
                    same,
                )
    for e in range(2):
        for cc in (0, 1):
            slot = x * 4 + e * 2 + cc
            wait(p_all.at[slot, high], pb_sem.at[slot])
            for d in (2, 1, 3):
                send(
                    lambda slot=slot, d=d: (
                        p_all.at[slot, high], p_all.at[slot, high], pb_sem.at[slot], dev(up(x, d, 4), y, z, c)
                    )
                )

    for d in (3, 5):
        slot = c * 8 + up(z, d, 8)
        q_wait(slot)
        q_send(slot, partner)
    slot = c * 8 + up(z, 4, 8)
    wait(q_all.at[slot, low], qh_sem.at[0])
    wait(q_all.at[slot, high], qh_sem.at[1])
    wait(qn_all.at[slot], qn_sem.at[slot])
    q_send(slot, partner)

    for e in range(4):
        for yy in (0, 1):
            for cc in (0, 1):
                slot = up(x, e, 4) * 4 + yy * 2 + cc
                pl.when(jnp.logical_not(jnp.logical_and(same, yl == yy)))(
                    lambda slot=slot: wait(p_all.at[slot, low], pa_sem.at[slot])
                )
                if e:
                    wait(p_all.at[slot, high], pb_sem.at[slot])
    for d in range(8):
        q_wait(other * 8 + up(z, d, 8))
    local_q.wait()
    wait(pn_all.at[0], pn_sem.at[0])

    scale = 2.0 / math.sqrt(width)
    g = (0.5 * scale) * loss_ref[0]
    columns = pn_all.shape[1]
    b = g * jnp.exp(TOP - pn_all[...])
    a_t = (g * jnp.exp(TOP - qn_all[...].reshape(16, 128))).T
    passages = p_all[...].reshape(columns, width)
    largest = jnp.zeros((8, 128), F32)
    column = lax.broadcasted_iota(jnp.int32, (ROWS, columns), 1) - lax.broadcasted_iota(jnp.int32, (ROWS, columns), 0)
    for chunk in range(4):
        rows = q_all[pl.ds(chunk * 4, 4)].reshape(4 * ROWS, width)
        scores = lax.dot_general(rows, passages, (((1,), (1,)), ((), ())), preferred_element_type=F32)
        terms = jnp.exp2(scores * (scale * LOG2E) - TOP * LOG2E)
        for k in range(4):
            slot = chunk * 4 + k
            first = ((x * 4 + yl * 2 + slot // 8) * 16 + (slot % 8) * 2 + yh) * ROWS - (z * 2 + c) * columns
            here = slice(k * ROWS, (k + 1) * ROWS)
            weights = terms[here] * (a_t[:ROWS, slot : slot + 1] + b) - jnp.where(column == first, 2.0 * g, 0.0)
            top = weights.astype(BF16)
            at = pl.ds(slot * ROWS, ROWS)
            w_hi[at, :] = top
            w_lo[at, :] = (weights - top.astype(F32)).astype(BF16)
            size = jnp.abs(weights)
            size = jnp.maximum(size[:HALF], size[HALF:])
            size = jnp.maximum(size[:8], size[8:])
            for j in range(columns // 128):
                largest = jnp.maximum(largest, size[:, j * 128 : (j + 1) * 128])
    mine = jnp.maximum(jnp.max(largest, axis=(0, 1), keepdims=True), 1e-30) * BOUND
    mine = jnp.broadcast_to(mine, (1, 128))
    sc_me[0] = mine
    send(lambda: (sc_me.at[0], sx_in.at[0], xs_sem.at[0], partner))
    for d in (2, 1, 3):
        send(lambda d=d: (sc_me.at[0], sx1_in.at[3 - d], rbs_sem.at[3 - d], dev(up(x, d, 4), y, z, c)))
    for yy in (0, 1):
        to = 2 * c + yy
        back = (y - to + 3) % 4
        send(
            lambda to=to, back=back: (sc_me.at[0], sy1_in.at[back], ras_sem.at[back], dev(x, to, z, c)),
            to != y,
        )

    def lane(row):
        return row[:, :1]

    inverse = lane(1.0 / mine)

    for chunk in range(2):
        at = pl.ds(pl.multiple_of(other * 8 * ROWS + chunk * 4 * ROWS, 4 * ROWS), 4 * ROWS)
        part = jnp.dot(w_hi[at, :], passages, preferred_element_type=F32)
        part += jnp.dot(w_lo[at, :], passages, preferred_element_type=F32)
        to = pl.ds(chunk * 4, 4)
        xq_out[to] = part.reshape(4, ROWS, width)
        send(lambda to=to, chunk=chunk: (xq_out.at[to], xq_in.at[to], xq_sem.at[chunk], partner))
    for chunk in range(2):
        at = pl.ds(pl.multiple_of(c * 8 * ROWS + chunk * 4 * ROWS, 4 * ROWS), 4 * ROWS)
        part = jnp.dot(w_hi[at, :], passages, preferred_element_type=F32)
        part += jnp.dot(w_lo[at, :], passages, preferred_element_type=F32)
        g_q[pl.ds(chunk * 4, 4)] = part.reshape(4, ROWS, width)

    queries = q_all[...].reshape(16 * ROWS, width)
    across = (((0,), (0,)), ((), ()))

    def passage_chunk(d):
        xm = up(x, d, 4)
        at = pl.ds(pl.multiple_of(xm * 4 * ROWS, 4 * ROWS), 4 * ROWS)
        part = lax.dot_general(w_hi[:, at], queries, across, preferred_element_type=F32)
        part += lax.dot_general(w_lo[:, at], queries, across, preferred_element_type=F32)
        part = part.reshape(2, 2, ROWS, width)
        g_p[xm] = part
        coded = encode(part, inverse)
        if d:
            pb_out[3 - d] = coded[:, :, HALF:]
            send(
                lambda: (pb_out.at[3 - d], pb_in.at[3 - d], rb_sem.at[3 - d], dev(xm, y, z, c)),
            )
        for yy in (0, 1):
            to = 2 * c + yy
            back = (y - to + 3) % 4
            pa_out[yy, xm] = coded[yy, :, :HALF]
            send(
                lambda yy=yy, to=to, back=back: (
                    pa_out.at[yy, xm], pa_in.at[back, xm], ra_sem.at[back, xm], dev(x, to, z, c)
                ),
                to != y,
            )

    passage_chunk(2)

    wait(sx_in.at[0], xs_sem.at[0])
    both = mine + sx_in[0]
    sc_q[0] = both
    for chunk in range(2):
        wait(xq_in.at[pl.ds(chunk * 4, 4)], xq_sem.at[chunk])
    for d in (1, 2, 6, 7):
        send(lambda d=d: (sc_q.at[0], sz_in.at[8 - d], zsc_sem.at[8 - d], dev(x, y, up(z, d, 8), c)))
    inverse_q = lane(1.0 / both)

    def column_sum(zz):
        return g_q[zz] + xq_in[zz]

    far = encode(column_sum(up(z, 4, 8)), inverse_q)
    zs1[4, low] = far[:HALF]
    zs1[4, high] = far[HALF:]
    for i, d in enumerate((5, 3)):
        zs1[i] = encode(column_sum(up(z, d, 8)), inverse_q)
    for i, d in enumerate((1, 7)):
        zs1[2 + i] = encode(column_sum(up(z, d, 8)), inverse_q)
    send(lambda: (zs1.at[4, low], zh_in.at[0], zh_sem.at[0], dev(x, y, up(z, 6, 8), c)))
    send(lambda: (zs1.at[4, high], zh_in.at[1], zh_sem.at[1], dev(x, y, up(z, 2, 8), c)))
    send(lambda: (zs1.at[0], zf_in.at[0], zf_sem.at[0], dev(x, y, up(z, 7, 8), c)))
    send(lambda: (zs1.at[1], zf_in.at[1], zf_sem.at[1], dev(x, y, up(z, 1, 8), c)))
    send(lambda: (zs1.at[2], zd_in.at[0], zd_sem.at[0], dev(x, y, up(z, 1, 8), c)))
    send(lambda: (zs1.at[3], zd_in.at[1], zd_sem.at[1], dev(x, y, up(z, 7, 8), c)))

    for d in (1, 3, 0):
        passage_chunk(d)

    for d in (1, 2, 6, 7):
        wait(sz_in.at[d], zsc_sem.at[d])
    for i in (0, 1):
        near, far_ = (1, 2) if i == 0 else (7, 6)
        wait(zf_in.at[i], zf_sem.at[i])
        wait(zh_in.at[i], zh_sem.at[i])
        total = both + sz_in[near] + sz_in[far_]
        sc_qr[i] = total
        value = column_sum(up(z, 6 if i == 0 else 2, 8)) + decode(zf_in[i], lane(sz_in[near]))
        extra = decode(zh_in[i], lane(sz_in[far_]))
        inv = lane(1.0 / total)
        first_half, second_half = value[:HALF], value[HALF:]
        if i == 0:
            first_half = first_half + extra
        else:
            second_half = second_half + extra
        zs2[i, low] = encode(first_half, inv)
        zs2[i, high] = encode(second_half, inv)
    for i in (0, 1):
        to = dev(x, y, up(z, 6 if i == 0 else 2, 8), c)
        send(lambda i=i, to=to: (sc_qr.at[i], sz2_in.at[i], zsc2_sem.at[i], to))
        send(lambda i=i, to=to: (zs2.at[i], z2_in.at[i], z2_sem.at[i], to))

    for d in (1, 2, 3):
        wait(sx1_in.at[d - 1], rbs_sem.at[d - 1])
        wait(pb_in.at[d - 1], rb_sem.at[d - 1])
    total_b = mine + sx1_in[0] + sx1_in[1] + sx1_in[2]
    sc_pb[0] = total_b
    inv_b = lane(1.0 / total_b)
    for yy in (0, 1):
        for cc in (0, 1):
            value = g_p[x, yy, cc, HALF:]
            for d in (1, 2, 3):
                value = value + decode(pb_in[d - 1, yy, cc], lane(sx1_in[d - 1]))
            fb_out[yy, cc] = encode(value, inv_b)
    for yy in (0, 1):
        for cc in (0, 1):
            to = 2 * c + yy
            back = (y - to + 4) % 4
            mine_too = jnp.logical_and(to == y, c == cc)

            @pl.when(mine_too)
            def _(yy=yy, cc=cc):
                fb_in[0] = fb_out[yy, cc]
                sfb_in[0] = total_b

            away = jnp.logical_not(mine_too)
            send(
                lambda to=to, back=back, cc=cc: (sc_pb.at[0], sfb_in.at[back], fbs_sem.at[back], dev(x, to, z, cc)), away
            )
            send(
                lambda to=to, back=back, yy=yy, cc=cc: (
                    fb_out.at[yy, cc], fb_in.at[back], fb_sem.at[back], dev(x, to, z, cc)
                ),
                away,
            )

    @pl.when(same)
    def _():
        for d in (1, 2, 3):
            wait(sy1_in.at[d - 1], ras_sem.at[d - 1])
        total_a = mine + sy1_in[0] + sy1_in[1] + sy1_in[2]
        sc_pa[0] = total_a
        inv_a = lane(1.0 / total_a)
        for e in (2, 1, 3, 0):
            xm = up(x, e, 4)
            for d in (1, 2, 3):
                wait(pa_in.at[d - 1, xm], ra_sem.at[d - 1, xm])
            for cc in (0, 1):
                value = g_p[xm, yl, cc, :HALF]
                for d in (1, 2, 3):
                    value = value + decode(pa_in[d - 1, xm, cc], lane(sy1_in[d - 1]))
                fa_out[e, cc] = encode(value, inv_a)
        fa_in[0] = fa_out[0, c]
        sfa_in[0] = total_a

    for e in (2, 1, 3):
        for cc in (0, 1):
            back = 4 - e
            send(
                lambda e=e, cc=cc, back=back: (sc_pa.at[0], sfa_in.at[back], fas_sem.at[back], dev(up(x, e, 4), y, z, cc)),
                same,
            )
            send(
                lambda e=e, cc=cc, back=back: (
                    fa_out.at[e, cc], fa_in.at[back], fa_sem.at[back], dev(up(x, e, 4), y, z, cc)
                ),
                same,
            )
    send(lambda: (sc_pa.at[0], sfa_in.at[0], fas_sem.at[0], partner), same)
    send(lambda: (fa_out.at[0, other], fa_in.at[0], fa_sem.at[0], partner), same)

    value = column_sum(z)
    for i, d in ((0, 7), (1, 1)):
        wait(zd_in.at[i], zd_sem.at[i])
        value = value + decode(zd_in[i], lane(sz_in[d]))
    for i in (0, 1):
        wait(sz2_in.at[i], zsc2_sem.at[i])
        wait(z2_in.at[i], z2_sem.at[i])
        value = value + decode(z2_in[i], lane(sz2_in[i]))
    oq_ref[...] = value

    for parts, scales, psem, sem, half in ((fb_in, sfb_in, fb_sem, fbs_sem, high), (fa_in, sfa_in, fa_sem, fas_sem, low)):
        for e in range(4):

            def arrived(e=e, parts=parts, scales=scales, psem=psem, sem=sem):
                wait(scales.at[e], sem.at[e])
                wait(parts.at[e], psem.at[e])

            if e:
                arrived()
            else:
                pl.when(jnp.logical_not(same))(arrived)
        value = decode(parts[0], lane(scales[0]))
        for e in (1, 2, 3):
            value = value + decode(parts[e], lane(scales[e]))
        op_ref[half, :] = value

    for make, when in pending:
        if when is None:
            make().wait_send()
        else:
            pl.when(when)(lambda make=make: make().wait_send())


N_SENDS = 200


def local(queries, passages, query_lognorm, passage_lognorm, loss_cotangent):
    width = queries.shape[1]
    columns = passage_lognorm.shape[0]
    dma = pltpu.SemaphoreType.DMA
    vm = pltpu.VMEM
    scratch = [
        vm((16, ROWS, width), BF16), vm((16, ROWS, width), BF16), vm((16, 1, 128), F32), vm((1, columns), F32),
        vm((16 * ROWS, columns), BF16), vm((16 * ROWS, columns), BF16),
        vm((8, ROWS, width), F32), vm((4, 2, 2, ROWS, width), F32),
        vm((8, ROWS, width), F32), vm((8, ROWS, width), F32),
        vm((5, ROWS, width), BF16), vm((2, ROWS, width), BF16), vm((2, ROWS, width), BF16),
        vm((2, ROWS, width), BF16), vm((2, HALF, width), BF16), vm((2, ROWS, width), BF16),
        vm((2, 4, 2, HALF, width), BF16), vm((3, 4, 2, HALF, width), BF16),
        vm((3, 2, 2, HALF, width), BF16), vm((3, 2, 2, HALF, width), BF16),
        vm((4, 2, HALF, width), BF16), vm((4, HALF, width), BF16),
        vm((2, 2, HALF, width), BF16), vm((4, HALF, width), BF16),
        *[vm((n, 1, 128), F32) for n in (1, 1, 2, 1, 1, 1, 8, 2, 3, 3, 4, 4)],
        dma((N_SENDS,)), dma((2,)), dma((16,)), dma((2,)), dma((16,)), dma((16,)), dma((16,)), dma((1,)),
        dma((2,)), dma((1,)), dma((2,)), dma((2,)), dma((2,)), dma((2,)), dma((8,)), dma((2,)),
        dma((3, 4)), dma((3,)), dma((3,)), dma((3,)), dma((4,)), dma((4,)), dma((4,)), dma((4,)),
    ]
    anywhere = pl.BlockSpec(memory_space=pl.ANY)
    out = jax.ShapeDtypeStruct(queries.shape, F32)

    def kernel(*refs):
        body(width, *refs)

    return pl.pallas_call(
        kernel,
        out_shape=(out, out),
        in_specs=[anywhere, anywhere, pl.BlockSpec(memory_space=pltpu.VMEM), anywhere] + [pl.BlockSpec(memory_space=pltpu.SMEM)],
        out_specs=[pl.BlockSpec(memory_space=pltpu.VMEM)] * 2,
        scratch_shapes=scratch,
        compiler_params=pltpu.CompilerParams(collective_id=0, has_side_effects=True),
    )(queries, passages, query_lognorm, passage_lognorm, loss_cotangent.reshape(1))


def solution(mesh):
    return jax.shard_map(
        local,
        mesh=mesh,
        in_specs=(
            P(("slab", "blk"), None),
            P(("blk", "slab"), None),
            P(("slab", "blk")),
            P("blk"),
            P(),
        ),
        out_specs=(P(("slab", "blk"), None), P(("blk", "slab"), None)),
        check_vma=False,
    )
```

```python
import math

import jax
import jax.numpy as jnp
from jax import lax
from jax.experimental import pallas as pl
from jax.experimental.pallas import tpu as pltpu
from jax.sharding import PartitionSpec as P

MESH = pl.DeviceIdType.MESH
F32, BF16 = jnp.float32, jnp.bfloat16
ROWS = 32
HALF = 16
BATCH = 8192
LOG2E = math.log2(math.e)
TOP = math.log(BATCH) + 3.5
BOUND = 512 * 6.0 * 2.0**-30
TINY = 1e-37


def encode(value, inverse):
    t = value * inverse
    u = t * jnp.abs(t)
    return (u * jnp.abs(u)).astype(BF16)


def decode(coded, scale):
    wide = coded.astype(F32)
    r = lax.rsqrt(jnp.maximum(jnp.abs(wide), TINY))
    return (wide * r) * (r * lax.rsqrt(r)) * scale


def body(
    width,
    q_in, p_in, qn_in, pn_in,
    oq_ref, op_ref,
    q_all, p_all, qn_all, pn_all,
    w_hi, w_lo, g_q, g_p, xq_out, xq_in,
    zs1, zs2, zd_in, zf_in, zh_in, z2_in,
    pa_out, pa_in, pb_out, pb_in,
    fa_out, fa_in, fb_out, fb_in,
    sc_me, sc_q, sc_qr, sc_pa, sc_pb, sx_in, sz_in, sz2_in, sy1_in, sx1_in, sfa_in, sfb_in,
    qn_smem, ssem, lsem, q_sem, qh_sem, qn_sem, pa_sem, pb_sem, pn_sem,
    xq_sem, xs_sem, zd_sem, zf_sem, zh_sem, z2_sem, zsc_sem, zsc2_sem,
    ra_sem, rb_sem, ras_sem, rbs_sem, fa_sem, fb_sem, fas_sem, fbs_sem,
):
    slab, blk = lax.axis_index("slab"), lax.axis_index("blk")

    def ring(value, size):
        return [value] + [lax.rem(value + d, size) for d in range(1, size)]

    x, c = lax.div(slab, 4), lax.rem(slab, 2)
    yl = lax.rem(lax.div(slab, 2), 2)
    z, yh = lax.div(blk, 2), lax.rem(blk, 2)
    y = yh * 2 + yl
    xs, ys, zs = ring(x, 4), ring(y, 4), ring(z, 8)
    in_row, in_block = yl * 2, z * 2 + yh
    y_row = [(lax.rem(yy, 2) * 2, z * 2 + lax.div(yy, 2)) for yy in ys]
    other = 1 - c
    same = c == yh
    partner = (slab + 1 - 2 * c, blk)

    def at_x(d, cc):
        return (xs[d] * 4 + in_row + cc, in_block)

    def at_y(d, cc):
        return (x * 4 + y_row[d][0] + cc, y_row[d][1])

    def at_z(d):
        return (slab, zs[d] * 2 + yh)

    def at_owner(yy, cc):
        return (x * 4 + yy * 2 + cc, z * 2 + c)

    pending = []
    count = [0]

    def send(build, when=None):
        index = count[0]
        count[0] += 1

        def make():
            src, dst, rsem, to = build()
            return pltpu.make_async_remote_copy(
                src_ref=src, dst_ref=dst, send_sem=ssem.at[index], recv_sem=rsem, device_id=to, device_id_type=MESH
            )

        if when is None:
            make().start()
        else:
            pl.when(when)(lambda: make().start())
        pending.append((make, when))

    def wait(dst, rsem):
        pltpu.make_async_remote_copy(
            src_ref=dst, dst_ref=dst, send_sem=lsem.at[0], recv_sem=rsem, device_id=partner, device_id_type=MESH
        ).wait_recv()

    def settle():
        for make, when in pending:
            if when is None:
                make().wait_send()
            else:
                pl.when(when)(lambda make=make: make().wait_send())
        pending.clear()

    barrier = pltpu.get_barrier_semaphore()
    peers = [at_z(d) for d in (2, 6)]
    peers += [at_x(d, cc) for d in (2, 1, 3) for cc in (0, 1)]
    peers += [at_y(d, cc) for d in (2, 1, 3) for cc in (0, 1)]
    peers += [at_z(d) for d in (1, 7)]
    peers += [partner]
    for peer in peers:
        pl.semaphore_signal(barrier, inc=1, device_id=peer, device_id_type=MESH)

    me_q = c * 8 + z
    low, high = pl.ds(0, HALF), pl.ds(HALF, HALF)
    norms = pltpu.make_async_copy(qn_in, qn_smem, lsem.at[2])
    norms.start()
    local_q = pltpu.make_async_copy(q_in, q_all.at[me_q], lsem.at[1])
    local_q.start()

    @pl.when(same)
    def _():
        pltpu.make_async_copy(p_in.at[low], p_all.at[slab, low], pa_sem.at[slab]).start()
        pltpu.make_async_copy(p_in.at[high], p_all.at[slab, high], pb_sem.at[slab]).start()
        pltpu.make_async_copy(pn_in, pn_all.at[0], pn_sem.at[0]).start()

    norms.wait()
    lanes = lax.broadcasted_iota(jnp.int32, (1, 128), 1)
    row = jnp.zeros((1, 128), F32)
    for i in range(ROWS):
        row = jnp.where(lanes == i, qn_smem[i], row)
    qn_all[me_q] = row
    pl.semaphore_wait(barrier, len(peers))

    def own(half, sem, to, when=None):
        send(lambda: (p_in.at[half], p_all.at[slab, half], sem.at[slab], to), when)

    def own_q(to):
        send(lambda: (q_in, q_all.at[me_q], q_sem.at[me_q], to))
        send(lambda: (qn_all.at[me_q], qn_all.at[me_q], qn_sem.at[me_q], to))

    apart = jnp.logical_not(same)
    own(low, pa_sem, partner, apart)
    own(high, pb_sem, partner, apart)
    for d in (2, 6):
        own_q(at_z(d))
    for d in (2, 1, 3):
        own(low, pa_sem, at_x(d, yh))
        own(high, pb_sem, at_y(d, yh))
    own_q(partner)
    for d in (1, 7):
        own_q(at_z(d))
    send(lambda: (pn_in, pn_all.at[0], pn_sem.at[0], at_y(2, c)), same)
    for d in (2, 1, 3):
        own(low, pa_sem, at_y(d, c), same)
        own(high, pb_sem, at_x(d, c), same)

    def relay_a(e, cc, mine=False):
        slot = xs[e] * 4 + in_row + cc

        @pl.when(same)
        def _():
            wait(p_all.at[slot, low], pa_sem.at[slot])

        for d in (2, 1, 3):
            send(lambda d=d: (p_all.at[slot, low], p_all.at[slot, low], pa_sem.at[slot], at_y(d, c)), same)

    def relay_b(yy, cc, when=None):
        slot = x * 4 + yy * 2 + cc
        if when is None:
            wait(p_all.at[slot, high], pb_sem.at[slot])
        else:
            pl.when(when)(lambda: wait(p_all.at[slot, high], pb_sem.at[slot]))
        for d in (2, 1, 3):
            send(lambda d=d: (p_all.at[slot, high], p_all.at[slot, high], pb_sem.at[slot], at_x(d, c)), when)

    relay_a(0, other)
    relay_b(yl, other, same)
    for e in (1, 3):
        for cc in (0, 1):
            relay_a(e, cc)
    for yy in (yl, 1 - yl):
        for cc in (0, 1):
            relay_b(yy, cc, apart if yy is yl else None)
    for cc in (0, 1):
        relay_a(2, cc)

    def q_wait(slot):
        wait(q_all.at[slot], q_sem.at[slot])
        wait(qn_all.at[slot], qn_sem.at[slot])

    def q_send(slot, to):
        send(lambda: (q_all.at[slot], q_all.at[slot], q_sem.at[slot], to))
        send(lambda: (qn_all.at[slot], qn_all.at[slot], qn_sem.at[slot], to))

    for d, near, far, half, hsem in ((6, 1, 2, low, 0), (2, 7, 6, high, 1)):
        slot = c * 8 + zs[d]
        q_wait(slot)
        send(
            lambda slot=slot, half=half, hsem=hsem, far=far: (
                q_all.at[slot, half], q_all.at[slot, half], qh_sem.at[hsem], at_z(far)
            )
        )
        if hsem == 0:
            send(lambda slot=slot, far=far: (qn_all.at[slot], qn_all.at[slot], qn_sem.at[slot], at_z(far)))
        q_send(slot, at_z(near))
        q_send(slot, partner)
    for d in (1, 7, 3, 5):
        slot = c * 8 + zs[d]
        q_wait(slot)
        q_send(slot, partner)
    slot = c * 8 + zs[4]
    wait(q_all.at[slot, low], qh_sem.at[0])
    wait(q_all.at[slot, high], qh_sem.at[1])
    wait(qn_all.at[slot], qn_sem.at[slot])
    q_send(slot, partner)

    for e in range(4):
        for yy in (yl, 1 - yl):
            for cc in (0, 1):
                slot = xs[e] * 4 + yy * 2 + cc

                def lower(slot=slot):
                    wait(p_all.at[slot, low], pa_sem.at[slot])

                if yy is not yl:
                    lower()
                else:
                    pl.when(apart)(lower)
                if e:
                    wait(p_all.at[slot, high], pb_sem.at[slot])

    @pl.when(same)
    def _():
        wait(p_all.at[slab, low], pa_sem.at[slab])
        wait(p_all.at[slab, high], pb_sem.at[slab])

    for d in range(8):
        q_wait(other * 8 + zs[d])
    local_q.wait()
    wait(pn_all.at[0], pn_sem.at[0])

    scale = 2.0 / math.sqrt(width)
    columns = pn_all.shape[1]
    b = jnp.exp(TOP - pn_all[...])
    a_t = jnp.exp(TOP - qn_all[...].reshape(16, 128)).T
    passages = p_all[...].reshape(columns, width)
    largest = jnp.zeros((8, 128), F32)
    column = lax.broadcasted_iota(jnp.int32, (ROWS, columns), 1) - lax.broadcasted_iota(jnp.int32, (ROWS, columns), 0)
    for chunk in range(4):
        rows = q_all[pl.ds(chunk * 4, 4)].reshape(4 * ROWS, width)
        scores = lax.dot_general(rows, passages, (((1,), (1,)), ((), ())), preferred_element_type=F32)
        terms = jnp.exp2(scores * (scale * LOG2E) - TOP * LOG2E)
        for k in range(4):
            slot = chunk * 4 + k
            first = ((x * 4 + yl * 2 + slot // 8) * 16 + (slot % 8) * 2 + yh) * ROWS - (z * 2 + c) * columns
            here = slice(k * ROWS, (k + 1) * ROWS)
            weights = terms[here] * (a_t[:ROWS, slot : slot + 1] + b) - jnp.where(column == first, 2.0, 0.0)
            top = weights.astype(BF16)
            at = pl.ds(slot * ROWS, ROWS)
            w_hi[at, :] = top
            w_lo[at, :] = (weights - top.astype(F32)).astype(BF16)
            size = jnp.abs(weights)
            size = jnp.maximum(size[:HALF], size[HALF:])
            size = jnp.maximum(size[:8], size[8:])
            for j in range(columns // 128):
                largest = jnp.maximum(largest, size[:, j * 128 : (j + 1) * 128])
    mine = jnp.maximum(jnp.max(largest, axis=(0, 1), keepdims=True), 1e-30) * BOUND
    mine = jnp.broadcast_to(mine, (1, 128))
    sc_me[0] = mine
    row_of = [2 * c + yy for yy in (0, 1)]
    far_row = [row != y for row in row_of]
    back_a = [lax.rem(y - row + 3 + 4, 4) for row in row_of]
    back_b = [lax.rem(y - row + 4, 4) for row in row_of]
    send(lambda: (sc_me.at[0], sx_in.at[0], xs_sem.at[0], partner))
    for d in (2, 1, 3):
        send(lambda d=d: (sc_me.at[0], sx1_in.at[3 - d], rbs_sem.at[3 - d], at_x(d, c)))
    for yy in (0, 1):
        send(
            lambda yy=yy: (sc_me.at[0], sy1_in.at[back_a[yy]], ras_sem.at[back_a[yy]], at_owner(yy, c)),
            far_row[yy],
        )

    def lane(row):
        return row[:, :1]

    inverse = lane(1.0 / mine)

    for chunk in range(2):
        at = pl.ds(pl.multiple_of(other * 8 * ROWS + chunk * 4 * ROWS, 4 * ROWS), 4 * ROWS)
        part = jnp.dot(w_hi[at, :], passages, preferred_element_type=F32)
        part += jnp.dot(w_lo[at, :], passages, preferred_element_type=F32)
        to = pl.ds(chunk * 4, 4)
        xq_out[to] = part.reshape(4, ROWS, width)
        send(lambda to=to, chunk=chunk: (xq_out.at[to], xq_in.at[to], xq_sem.at[chunk], partner))
    for chunk in range(2):
        at = pl.ds(pl.multiple_of(c * 8 * ROWS + chunk * 4 * ROWS, 4 * ROWS), 4 * ROWS)
        part = jnp.dot(w_hi[at, :], passages, preferred_element_type=F32)
        part += jnp.dot(w_lo[at, :], passages, preferred_element_type=F32)
        g_q[pl.ds(chunk * 4, 4)] = part.reshape(4, ROWS, width)

    queries = q_all[...].reshape(16 * ROWS, width)
    across = (((0,), (0,)), ((), ()))

    def passage_chunk(d):
        xm = xs[d]
        at = pl.ds(pl.multiple_of(xm * 4 * ROWS, 4 * ROWS), 4 * ROWS)
        part = lax.dot_general(w_hi[:, at], queries, across, preferred_element_type=F32)
        part += lax.dot_general(w_lo[:, at], queries, across, preferred_element_type=F32)
        part = part.reshape(2, 2, ROWS, width)
        g_p[xm] = part
        for yy in (0, 1):
            coded = encode(part[yy], inverse)
            pa_out[yy, xm] = coded[:, :HALF]
            if d:
                pb_out[3 - d, yy] = coded[:, HALF:]
                send(lambda yy=yy: (pb_out.at[3 - d, yy], pb_in.at[3 - d, yy], rb_sem.at[3 - d, yy], at_x(d, c)))
            send(
                lambda yy=yy: (pa_out.at[yy, xm], pa_in.at[back_a[yy], xm], ra_sem.at[back_a[yy], xm], at_owner(yy, c)),
                far_row[yy],
            )

    passage_chunk(2)

    wait(sx_in.at[0], xs_sem.at[0])
    both = mine + sx_in[0]
    sc_q[0] = both
    for chunk in range(2):
        wait(xq_in.at[pl.ds(chunk * 4, 4)], xq_sem.at[chunk])
    for d in (1, 2, 6, 7):
        send(lambda d=d: (sc_q.at[0], sz_in.at[8 - d], zsc_sem.at[8 - d], at_z(d)))
    inverse_q = lane(1.0 / both)

    def column_sum(zz):
        return g_q[zz] + xq_in[zz]

    far = encode(column_sum(zs[4]), inverse_q)
    zs1[4, low] = far[:HALF]
    zs1[4, high] = far[HALF:]
    for i, d in enumerate((5, 3)):
        zs1[i] = encode(column_sum(zs[d]), inverse_q)
    for i, d in enumerate((1, 7)):
        zs1[2 + i] = encode(column_sum(zs[d]), inverse_q)
    send(lambda: (zs1.at[4, low], zh_in.at[0], zh_sem.at[0], at_z(6)))
    send(lambda: (zs1.at[4, high], zh_in.at[1], zh_sem.at[1], at_z(2)))
    send(lambda: (zs1.at[0], zf_in.at[0], zf_sem.at[0], at_z(7)))
    send(lambda: (zs1.at[1], zf_in.at[1], zf_sem.at[1], at_z(1)))
    send(lambda: (zs1.at[2], zd_in.at[0], zd_sem.at[0], at_z(1)))
    send(lambda: (zs1.at[3], zd_in.at[1], zd_sem.at[1], at_z(7)))

    for d in (1, 3, 0):
        passage_chunk(d)

    settle()

    def relay_rows():
        for d in (1, 2, 6, 7):
            wait(sz_in.at[d], zsc_sem.at[d])
        for i in (0, 1):
            near, far_ = (1, 2) if i == 0 else (7, 6)
            to = at_z(6 if i == 0 else 2)
            wait(zh_in.at[i], zh_sem.at[i])
            wait(zf_in.at[i], zf_sem.at[i])
            total = both + sz_in[near] + sz_in[far_]
            sc_qr[i] = total
            value = column_sum(zs[6 if i == 0 else 2]) + decode(zf_in[i], lane(sz_in[near]))
            extra = decode(zh_in[i], lane(sz_in[far_]))
            inv = lane(1.0 / total)
            first_half, second_half = value[:HALF], value[HALF:]
            if i == 0:
                first_half = first_half + extra
            else:
                second_half = second_half + extra
            zs2[i, low] = encode(first_half, inv)
            zs2[i, high] = encode(second_half, inv)
            send(lambda i=i, to=to: (sc_qr.at[i], sz2_in.at[i], zsc2_sem.at[i], to))
            send(lambda i=i, to=to: (zs2.at[i], z2_in.at[i], z2_sem.at[i], to))

    total_b = []

    def relay_upper(yy):
        if not total_b:
            for d in (1, 2, 3):
                wait(sx1_in.at[d - 1], rbs_sem.at[d - 1])
            total_b.append(mine + sx1_in[0] + sx1_in[1] + sx1_in[2])
            sc_pb[0] = total_b[0]
        inv_b = lane(1.0 / total_b[0])
        for d in (2, 1, 3):
            wait(pb_in.at[d - 1, yy], rb_sem.at[d - 1, yy])
        for cc in (0, 1):
            value = g_p[x, yy, cc, HALF:]
            for d in (2, 1, 3):
                value = value + decode(pb_in[d - 1, yy, cc], lane(sx1_in[d - 1]))
            fb_out[yy, cc] = encode(value, inv_b)
        for cc in (0, 1):
            mine_too = jnp.logical_and(jnp.logical_not(far_row[yy]), c == cc)

            @pl.when(mine_too)
            def _(cc=cc):
                fb_in[0] = fb_out[yy, cc]
                sfb_in[0] = total_b[0]

            away = jnp.logical_not(mine_too)
            back, to = back_b[yy], at_owner(yy, cc)
            send(lambda: (sc_pb.at[0], sfb_in.at[back], fbs_sem.at[back], to), away)
            send(lambda cc=cc, back=back, to=to: (fb_out.at[yy, cc], fb_in.at[back], fb_sem.at[back], to), away)

    def relay_lower(e):
        xm = xs[e]

        @pl.when(same)
        def _():
            if e == 2:
                for d in (1, 2, 3):
                    wait(sy1_in.at[d - 1], ras_sem.at[d - 1])
                sc_pa[0] = mine + sy1_in[0] + sy1_in[1] + sy1_in[2]
            inv_a = lane(1.0 / sc_pa[0])
            for d in (1, 2, 3):
                wait(pa_in.at[d - 1, xm], ra_sem.at[d - 1, xm])
            for cc in (0, 1):
                value = g_p[xm, yl, cc, :HALF]
                for d in (1, 2, 3):
                    value = value + decode(pa_in[d - 1, xm, cc], lane(sy1_in[d - 1]))
                fa_out[e, cc] = encode(value, inv_a)
            if e == 0:
                fa_in[0] = fa_out[0, c]
                sfa_in[0] = sc_pa[0]

        if e:
            back = 4 - e
            for cc in (0, 1):
                send(lambda cc=cc: (sc_pa.at[0], sfa_in.at[back], fas_sem.at[back], at_x(e, cc)), same)
                send(lambda cc=cc: (fa_out.at[e, cc], fa_in.at[back], fa_sem.at[back], at_x(e, cc)), same)
        else:
            send(lambda: (sc_pa.at[0], sfa_in.at[0], fas_sem.at[0], partner), same)
            send(lambda: (fa_out.at[0, other], fa_in.at[0], fa_sem.at[0], partner), same)

    relay_lower(2)
    relay_lower(1)
    relay_rows()
    relay_upper(0)
    relay_lower(3)
    relay_upper(1)
    relay_lower(0)

    value = column_sum(z)
    for i, d in ((0, 7), (1, 1)):
        wait(zd_in.at[i], zd_sem.at[i])
        value = value + decode(zd_in[i], lane(sz_in[d]))
    for i in (0, 1):
        wait(sz2_in.at[i], zsc2_sem.at[i])
        wait(z2_in.at[i], z2_sem.at[i])
        value = value + decode(z2_in[i], lane(sz2_in[i]))
    oq_ref[...] = value

    for parts, scales, psem, sem, half in ((fb_in, sfb_in, fb_sem, fbs_sem, high), (fa_in, sfa_in, fa_sem, fas_sem, low)):
        for e in range(4):

            def arrived(e=e, parts=parts, scales=scales, psem=psem, sem=sem):
                wait(scales.at[e], sem.at[e])
                wait(parts.at[e], psem.at[e])

            if e:
                arrived()
            else:
                pl.when(jnp.logical_not(same))(arrived)
        value = decode(parts[0], lane(scales[0]))
        for e in (1, 2, 3):
            value = value + decode(parts[e], lane(scales[e]))
        op_ref[half, :] = value

    settle()


N_SENDS = 220
VMEM_LIMIT = 20 * 2**20


def local(queries, passages, query_lognorm, passage_lognorm, loss_cotangent):
    width = queries.shape[1]
    columns = passage_lognorm.shape[0]
    dma = pltpu.SemaphoreType.DMA
    vm = pltpu.VMEM
    scratch = [
        vm((16, ROWS, width), BF16), vm((16, ROWS, width), BF16), vm((16, 1, 128), F32), vm((1, columns), F32),
        vm((16 * ROWS, columns), BF16), vm((16 * ROWS, columns), BF16),
        vm((8, ROWS, width), F32), vm((4, 2, 2, ROWS, width), F32),
        vm((8, ROWS, width), F32), vm((8, ROWS, width), F32),
        vm((5, ROWS, width), BF16), vm((2, ROWS, width), BF16), vm((2, ROWS, width), BF16),
        vm((2, ROWS, width), BF16), vm((2, HALF, width), BF16), vm((2, ROWS, width), BF16),
        vm((2, 4, 2, HALF, width), BF16), vm((3, 4, 2, HALF, width), BF16),
        vm((3, 2, 2, HALF, width), BF16), vm((3, 2, 2, HALF, width), BF16),
        vm((4, 2, HALF, width), BF16), vm((4, HALF, width), BF16),
        vm((2, 2, HALF, width), BF16), vm((4, HALF, width), BF16),
        *[vm((n, 1, 128), F32) for n in (1, 1, 2, 1, 1, 1, 8, 2, 3, 3, 4, 4)],
        pltpu.SMEM((ROWS,), F32), dma((N_SENDS,)), dma((3,)), dma((16,)), dma((2,)), dma((16,)), dma((16,)), dma((16,)), dma((1,)),
        dma((2,)), dma((1,)), dma((2,)), dma((2,)), dma((2,)), dma((2,)), dma((8,)), dma((2,)),
        dma((3, 4)), dma((3, 2)), dma((3,)), dma((3,)), dma((4,)), dma((4,)), dma((4,)), dma((4,)),
    ]
    out = jax.ShapeDtypeStruct(queries.shape, F32)
    vmem = pl.BlockSpec(memory_space=pltpu.VMEM)

    def kernel(*refs):
        body(width, *refs)

    sums = pl.pallas_call(
        kernel,
        out_shape=(out, out),
        in_specs=[pl.BlockSpec(memory_space=pltpu.HBM)] * 4,
        out_specs=[vmem] * 2,
        scratch_shapes=scratch,
        compiler_params=pltpu.CompilerParams(collective_id=0, has_side_effects=True, vmem_limit_bytes=VMEM_LIMIT),
    )(*[pltpu.with_memory_space_constraint(v, pltpu.HBM) for v in (queries, passages, query_lognorm, passage_lognorm)])

    factor = loss_cotangent * (1.0 / math.sqrt(width))
    return sums[0] * factor, sums[1] * factor


def solution(mesh):
    return jax.shard_map(
        local,
        mesh=mesh,
        in_specs=(
            P(("slab", "blk"), None),
            P(("blk", "slab"), None),
            P(("slab", "blk")),
            P("blk"),
            P(),
        ),
        out_specs=(P(("slab", "blk"), None), P(("blk", "slab"), None)),
        check_vma=False,
    )
```

```python
import math

import jax
import jax.numpy as jnp
from jax import lax
from jax.experimental import pallas as pl
from jax.experimental.pallas import tpu as pltpu
from jax.sharding import PartitionSpec as P

MESH = pl.DeviceIdType.MESH
F32, BF16 = jnp.float32, jnp.bfloat16
ROWS = 32
HALF = 16
BATCH = 8192
LOG2E = math.log2(math.e)
TOP = math.log(BATCH) + 3.5
BOUND = 512 * 6.0 * 2.0**-30
TINY = 1e-37


def encode(value, inverse):
    t = value * inverse
    u = t * jnp.abs(t)
    return (u * jnp.abs(u)).astype(BF16)


def decode(coded, scale):
    wide = coded.astype(F32)
    r = lax.rsqrt(jnp.maximum(jnp.abs(wide), TINY))
    return (wide * r) * (r * lax.rsqrt(r)) * scale


def body(
    width,
    q_in, p_in, qn_in, pn_in,
    oq_ref, op_ref,
    q_all, p_all, p_own, qn_all, pn_all,
    w_hi, w_lo, g_q, g_p, xq_out, xq_in,
    zs1, zs2, zd_in, zf_in, zh_in, z2_in,
    pa_out, pa_in, pb_out, pb_in,
    fa_out, fa_in, fb_out, fb_in,
    sc_me, sc_q, sc_qr, sc_pa, sc_pb, sx_in, sz_in, sz2_in, sy1_in, sx1_in, sfa_in, sfb_in,
    qn_smem, ssem, lsem, q_sem, qn_sem, pa_sem, pb_sem, pn_sem,
    xq_sem, xs_sem, zd_sem, zf_sem, zh_sem, z2_sem, zsc_sem, zsc2_sem,
    ra_sem, rb_sem, ras_sem, rbs_sem, fa_sem, fb_sem, fas_sem, fbs_sem,
):
    slab, blk = lax.axis_index("slab"), lax.axis_index("blk")

    def ring(value, size):
        return [value] + [lax.rem(value + d, size) for d in range(1, size)]

    x, c = lax.div(slab, 4), lax.rem(slab, 2)
    yl = lax.rem(lax.div(slab, 2), 2)
    z, yh = lax.div(blk, 2), lax.rem(blk, 2)
    y = yh * 2 + yl
    xs, ys, zs = ring(x, 4), ring(y, 4), ring(z, 8)
    in_row, in_block = yl * 2, z * 2 + yh
    y_row = [(lax.rem(yy, 2) * 2, z * 2 + lax.div(yy, 2)) for yy in ys]
    other = 1 - c
    same = c == yh
    partner = (slab + 1 - 2 * c, blk)

    def at_x(d, cc):
        return (xs[d] * 4 + in_row + cc, in_block)

    def at_y(d, cc):
        return (x * 4 + y_row[d][0] + cc, y_row[d][1])

    def at_z(d):
        return (slab, zs[d] * 2 + yh)

    def at_owner(yy, cc):
        return (x * 4 + yy * 2 + cc, z * 2 + c)

    pending = []
    count = [0]
    free = []

    def send(build, when=None):
        if free:
            index = free.pop(0)
        else:
            index = count[0]
            count[0] += 1
            assert index < N_SENDS

        def make():
            src, dst, rsem, to = build()
            return pltpu.make_async_remote_copy(
                src_ref=src, dst_ref=dst, send_sem=ssem.at[index], recv_sem=rsem, device_id=to, device_id_type=MESH
            )

        if when is None:
            make().start()
        else:
            pl.when(when)(lambda: make().start())
        pending.append((make, when, index))

    def wait(dst, rsem):
        pltpu.make_async_remote_copy(
            src_ref=dst, dst_ref=dst, send_sem=lsem.at[0], recv_sem=rsem, device_id=partner, device_id_type=MESH
        ).wait_recv()

    def settle(first=None):
        first = len(pending) if first is None else first
        for make, when, index in pending[:first]:
            if when is None:
                make().wait_send()
            else:
                pl.when(when)(lambda make=make: make().wait_send())
            free.append(index)
        del pending[:first]

    me_q = c * 8 + z
    low, high = pl.ds(0, HALF), pl.ds(HALF, HALF)
    halves = (low, high)
    norms = pltpu.make_async_copy(qn_in, qn_smem, lsem.at[2])
    local_q = pltpu.make_async_copy(q_in, q_all.at[me_q], lsem.at[1])
    local_p = pltpu.make_async_copy(p_in, p_own, lsem.at[3])
    local_p.start()
    local_q.start()
    norms.start()
    barrier = pltpu.get_barrier_semaphore()
    peers = [at_x(2, cc) for cc in (0, 1)] + [at_y(2, cc) for cc in (0, 1)]
    peers += [at_x(d, cc) for d in (1, 3) for cc in (0, 1)]
    peers += [at_y(d, cc) for d in (1, 3) for cc in (0, 1)]
    peers += [at_z(d) for d in Z_PEERS]
    peers += [partner]
    for peer in peers:
        pl.semaphore_signal(barrier, inc=1, device_id=peer, device_id_type=MESH)

    @pl.when(same)
    def _():
        pltpu.make_async_copy(p_in.at[low], p_all.at[slab, low], pa_sem.at[slab]).start()
        pltpu.make_async_copy(p_in.at[high], p_all.at[slab, high], pb_sem.at[slab]).start()
        pltpu.make_async_copy(pn_in, pn_all.at[0], pn_sem.at[0]).start()

    local_p.wait()
    local_q.wait()
    pl.semaphore_wait(barrier, len(peers))

    def own(half, sem, to, when=None):
        send(lambda: (p_own.at[half], p_all.at[slab, half], sem.at[slab], to), when)

    def q_send(slot, h, to):
        send(lambda: (q_all.at[slot, halves[h]], q_all.at[slot, halves[h]], q_sem.at[slot, h], to))

    def n_send(slot, to):
        send(lambda: (qn_all.at[slot], qn_all.at[slot], qn_sem.at[slot], to))

    apart = jnp.logical_not(same)
    own(low, pa_sem, partner, apart)
    own(high, pb_sem, partner, apart)
    q_send(me_q, 0, at_z(2))
    q_send(me_q, 1, at_z(6))
    for d in (1, 3):
        own(low, pa_sem, at_x(d, yh))
        own(high, pb_sem, at_y(d, yh))
    q_send(me_q, 1, at_z(2))
    q_send(me_q, 0, at_z(6))
    for d in (1, 7):
        q_send(me_q, 0, at_z(d))
        q_send(me_q, 1, at_z(d))
    own(low, pa_sem, at_x(2, yh))
    own(high, pb_sem, at_y(2, yh))
    for d in (1, 3, 2):
        own(low, pa_sem, at_y(d, c), same)
        own(high, pb_sem, at_x(d, c), same)
    q_send(me_q, 0, partner)
    q_send(me_q, 1, partner)
    send(lambda: (pn_in, pn_all.at[0], pn_sem.at[0], at_y(2, c)), same)
    norms.wait()
    lanes = lax.broadcasted_iota(jnp.int32, (1, 128), 1)
    row = jnp.zeros((1, 128), F32)
    for i in range(ROWS):
        row = jnp.where(lanes == i, qn_smem[i], row)
    qn_all[me_q] = row

    def relay_a(e, cc):
        slot = xs[e] * 4 + in_row + cc

        @pl.when(same)
        def _():
            wait(p_all.at[slot, low], pa_sem.at[slot])

        for d in (1, 3, 2):
            send(lambda d=d: (p_all.at[slot, low], p_all.at[slot, low], pa_sem.at[slot], at_y(d, c)), same)

    def relay_b(yy, cc, when=None):
        slot = x * 4 + yy * 2 + cc
        if when is None:
            wait(p_all.at[slot, high], pb_sem.at[slot])
        else:
            pl.when(when)(lambda: wait(p_all.at[slot, high], pb_sem.at[slot]))
        for d in (1, 3, 2):
            send(lambda d=d: (p_all.at[slot, high], p_all.at[slot, high], pb_sem.at[slot], at_x(d, c)), when)

    def q_wait(slot, h):
        wait(q_all.at[slot, halves[h]], q_sem.at[slot, h])

    def n_wait(slot):
        wait(qn_all.at[slot], qn_sem.at[slot])

    def hop(k, h, to_right):
        slot = c * 8 + zs[8 - k if to_right else k]
        q_wait(slot, h)
        if k == 2:
            if h == (0 if to_right else 1):
                q_send(slot, h, at_z(2 if to_right else 6))
            q_send(slot, h, at_z(1 if to_right else 7))
        q_send(slot, h, partner)

    def norm_hop(k, to_right):
        slot = c * 8 + zs[8 - k if to_right else k]
        n_wait(slot)
        if k == 2:
            if to_right:
                n_send(slot, at_z(2))
            n_send(slot, at_z(1 if to_right else 7))
        n_send(slot, partner)

    for to in (at_z(2), at_z(6), at_z(1), at_z(7), partner):
        n_send(me_q, to)
    early = len(pending)
    relay_a(0, other)
    relay_b(yl, other, same)
    for e in (1, 3):
        for cc in (0, 1):
            relay_a(e, cc)
    for yy in (yl, 1 - yl):
        for cc in (0, 1):
            relay_b(yy, cc, apart if yy is yl else None)
    hop(2, 0, True)
    hop(2, 1, False)
    for cc in (0, 1):
        relay_a(2, cc)
    hop(2, 1, True)
    hop(2, 0, False)
    norm_hop(2, True)
    norm_hop(2, False)
    settle(early)
    for k in (1, 3):
        for right in (True, False):
            for h in (0, 1) if right else (1, 0):
                hop(k, h, right)
            norm_hop(k, right)
    hop(4, 0, True)
    hop(4, 1, False)
    norm_hop(4, True)

    for e in range(4):
        for yy in (yl, 1 - yl):
            for cc in (0, 1):
                slot = xs[e] * 4 + yy * 2 + cc

                def lower(slot=slot):
                    wait(p_all.at[slot, low], pa_sem.at[slot])

                if yy is not yl:
                    lower()
                else:
                    pl.when(apart)(lower)
                if e:
                    wait(p_all.at[slot, high], pb_sem.at[slot])

    @pl.when(same)
    def _():
        wait(p_all.at[slab, low], pa_sem.at[slab])
        wait(p_all.at[slab, high], pb_sem.at[slab])

    for d in (0, 1, 7, 2, 6, 3, 5, 4):
        slot = other * 8 + zs[d]
        q_wait(slot, 0)
        q_wait(slot, 1)
        n_wait(slot)
    wait(pn_all.at[0], pn_sem.at[0])

    scale = 2.0 / math.sqrt(width)
    columns = pn_all.shape[1]
    b = jnp.exp(TOP - pn_all[...])
    a_t = jnp.exp(TOP - qn_all[...].reshape(16, 128)).T
    passages = p_all[...].reshape(columns, width)
    largest = jnp.zeros((8, 128), F32)
    column = lax.broadcasted_iota(jnp.int32, (ROWS, columns), 1) - lax.broadcasted_iota(jnp.int32, (ROWS, columns), 0)
    for chunk in range(4):
        rows = q_all[pl.ds(chunk * 4, 4)].reshape(4 * ROWS, width)
        scores = lax.dot_general(rows, passages, (((1,), (1,)), ((), ())), preferred_element_type=F32)
        terms = jnp.exp2(scores * (scale * LOG2E) - TOP * LOG2E)
        for k in range(4):
            slot = chunk * 4 + k
            first = ((x * 4 + yl * 2 + slot // 8) * 16 + (slot % 8) * 2 + yh) * ROWS - (z * 2 + c) * columns
            here = slice(k * ROWS, (k + 1) * ROWS)
            weights = terms[here] * (a_t[:ROWS, slot : slot + 1] + b) - jnp.where(column == first, 2.0, 0.0)
            top = weights.astype(BF16)
            at = pl.ds(slot * ROWS, ROWS)
            w_hi[at, :] = top
            w_lo[at, :] = (weights - top.astype(F32)).astype(BF16)
            size = jnp.abs(weights)
            size = jnp.maximum(size[:HALF], size[HALF:])
            size = jnp.maximum(size[:8], size[8:])
            for j in range(columns // 128):
                largest = jnp.maximum(largest, size[:, j * 128 : (j + 1) * 128])
    mine = jnp.maximum(jnp.max(largest, axis=(0, 1), keepdims=True), 1e-30) * BOUND
    mine = jnp.broadcast_to(mine, (1, 128))
    settle()
    sc_me[0] = mine
    row_of = [2 * c + yy for yy in (0, 1)]
    far_row = [row != y for row in row_of]
    back_a = [lax.rem(y - row + 3 + 4, 4) for row in row_of]
    back_b = [lax.rem(y - row + 4, 4) for row in row_of]
    send(lambda: (sc_me.at[0], sx_in.at[0], xs_sem.at[0], partner))
    for d in (2, 1, 3):
        send(lambda d=d: (sc_me.at[0], sx1_in.at[3 - d], rbs_sem.at[3 - d], at_x(d, c)))
    for yy in (0, 1):
        send(
            lambda yy=yy: (sc_me.at[0], sy1_in.at[back_a[yy]], ras_sem.at[back_a[yy]], at_owner(yy, c)),
            far_row[yy],
        )

    def lane(row):
        return row[:, :1]

    inverse = lane(1.0 / mine)

    for chunk in range(2):
        at = pl.ds(pl.multiple_of(other * 8 * ROWS + chunk * 4 * ROWS, 4 * ROWS), 4 * ROWS)
        part = jnp.dot(w_hi[at, :], passages, preferred_element_type=F32)
        part += jnp.dot(w_lo[at, :], passages, preferred_element_type=F32)
        to = pl.ds(chunk * 4, 4)
        xq_out[to] = part.reshape(4, ROWS, width)
        send(lambda to=to, chunk=chunk: (xq_out.at[to], xq_in.at[to], xq_sem.at[chunk], partner))
    for chunk in range(2):
        at = pl.ds(pl.multiple_of(c * 8 * ROWS + chunk * 4 * ROWS, 4 * ROWS), 4 * ROWS)
        part = jnp.dot(w_hi[at, :], passages, preferred_element_type=F32)
        part += jnp.dot(w_lo[at, :], passages, preferred_element_type=F32)
        g_q[pl.ds(chunk * 4, 4)] = part.reshape(4, ROWS, width)

    queries = q_all[...].reshape(16 * ROWS, width)
    across = (((0,), (0,)), ((), ()))

    def passage_chunk(d):
        xm = xs[d]
        at = pl.ds(pl.multiple_of(xm * 4 * ROWS, 4 * ROWS), 4 * ROWS)
        part = lax.dot_general(w_hi[:, at], queries, across, preferred_element_type=F32)
        part += lax.dot_general(w_lo[:, at], queries, across, preferred_element_type=F32)
        part = part.reshape(2, 2, ROWS, width)
        g_p[xm] = part
        for yy in (0, 1):
            coded = encode(part[yy], inverse)
            pa_out[yy, xm] = coded[:, :HALF]
            if d:
                pb_out[3 - d, yy] = coded[:, HALF:]
                send(lambda yy=yy: (pb_out.at[3 - d, yy], pb_in.at[3 - d, yy], rb_sem.at[3 - d, yy], at_x(d, c)))
            send(
                lambda yy=yy: (pa_out.at[yy, xm], pa_in.at[back_a[yy], xm], ra_sem.at[back_a[yy], xm], at_owner(yy, c)),
                far_row[yy],
            )

    passage_chunk(2)

    wait(sx_in.at[0], xs_sem.at[0])
    both = mine + sx_in[0]
    sc_q[0] = both
    for chunk in range(2):
        wait(xq_in.at[pl.ds(chunk * 4, 4)], xq_sem.at[chunk])
    for d in (1, 2, 6, 7):
        send(lambda d=d: (sc_q.at[0], sz_in.at[8 - d], zsc_sem.at[8 - d], at_z(d)))
    inverse_q = lane(1.0 / both)

    def column_sum(zz):
        return g_q[zz] + xq_in[zz]

    far = encode(column_sum(zs[4]), inverse_q)
    zs1[4, low] = far[:HALF]
    zs1[4, high] = far[HALF:]
    for i, d in enumerate((5, 3)):
        zs1[i] = encode(column_sum(zs[d]), inverse_q)
    for i, d in enumerate((1, 7)):
        zs1[2 + i] = encode(column_sum(zs[d]), inverse_q)
    send(lambda: (zs1.at[4, low], zh_in.at[0], zh_sem.at[0], at_z(6)))
    send(lambda: (zs1.at[4, high], zh_in.at[1], zh_sem.at[1], at_z(2)))
    send(lambda: (zs1.at[0], zf_in.at[0], zf_sem.at[0], at_z(7)))
    send(lambda: (zs1.at[1], zf_in.at[1], zf_sem.at[1], at_z(1)))
    send(lambda: (zs1.at[2], zd_in.at[0], zd_sem.at[0], at_z(1)))
    send(lambda: (zs1.at[3], zd_in.at[1], zd_sem.at[1], at_z(7)))

    for d in (1, 3, 0):
        passage_chunk(d)

    settle()

    def relay_rows():
        for d in (1, 2, 6, 7):
            wait(sz_in.at[d], zsc_sem.at[d])
        for i in (0, 1):
            near, far_ = (1, 2) if i == 0 else (7, 6)
            to = at_z(6 if i == 0 else 2)
            wait(zh_in.at[i], zh_sem.at[i])
            wait(zf_in.at[i], zf_sem.at[i])
            total = both + sz_in[near] + sz_in[far_]
            sc_qr[i] = total
            value = column_sum(zs[6 if i == 0 else 2]) + decode(zf_in[i], lane(sz_in[near]))
            extra = decode(zh_in[i], lane(sz_in[far_]))
            inv = lane(1.0 / total)
            first_half, second_half = value[:HALF], value[HALF:]
            if i == 0:
                first_half = first_half + extra
            else:
                second_half = second_half + extra
            zs2[i, low] = encode(first_half, inv)
            zs2[i, high] = encode(second_half, inv)
            send(lambda i=i, to=to: (sc_qr.at[i], sz2_in.at[i], zsc2_sem.at[i], to))
            send(lambda i=i, to=to: (zs2.at[i], z2_in.at[i], z2_sem.at[i], to))

    total_b = []

    def relay_upper(yy):
        if not total_b:
            for d in (1, 2, 3):
                wait(sx1_in.at[d - 1], rbs_sem.at[d - 1])
            total_b.append(mine + sx1_in[0] + sx1_in[1] + sx1_in[2])
            sc_pb[0] = total_b[0]
        inv_b = lane(1.0 / total_b[0])
        for d in (2, 1, 3):
            wait(pb_in.at[d - 1, yy], rb_sem.at[d - 1, yy])
        for cc in (0, 1):
            value = g_p[x, yy, cc, HALF:]
            for d in (2, 1, 3):
                value = value + decode(pb_in[d - 1, yy, cc], lane(sx1_in[d - 1]))
            fb_out[yy, cc] = encode(value, inv_b)
        for cc in (0, 1):
            mine_too = jnp.logical_and(jnp.logical_not(far_row[yy]), c == cc)

            @pl.when(mine_too)
            def _(cc=cc):
                fb_in[0] = fb_out[yy, cc]
                sfb_in[0] = total_b[0]

            away = jnp.logical_not(mine_too)
            back, to = back_b[yy], at_owner(yy, cc)
            send(lambda: (sc_pb.at[0], sfb_in.at[back], fbs_sem.at[back], to), away)
            send(lambda cc=cc, back=back, to=to: (fb_out.at[yy, cc], fb_in.at[back], fb_sem.at[back], to), away)

    def relay_lower(e):
        xm = xs[e]

        @pl.when(same)
        def _():
            if e == 2:
                for d in (1, 2, 3):
                    wait(sy1_in.at[d - 1], ras_sem.at[d - 1])
                sc_pa[0] = mine + sy1_in[0] + sy1_in[1] + sy1_in[2]
            inv_a = lane(1.0 / sc_pa[0])
            for d in (1, 2, 3):
                wait(pa_in.at[d - 1, xm], ra_sem.at[d - 1, xm])
            for cc in (0, 1):
                value = g_p[xm, yl, cc, :HALF]
                for d in (1, 2, 3):
                    value = value + decode(pa_in[d - 1, xm, cc], lane(sy1_in[d - 1]))
                fa_out[e, cc] = encode(value, inv_a)
            if e == 0:
                fa_in[0] = fa_out[0, c]
                sfa_in[0] = sc_pa[0]

        if e:
            back = 4 - e
            for cc in (0, 1):
                send(lambda cc=cc: (sc_pa.at[0], sfa_in.at[back], fas_sem.at[back], at_x(e, cc)), same)
                send(lambda cc=cc: (fa_out.at[e, cc], fa_in.at[back], fa_sem.at[back], at_x(e, cc)), same)
        else:
            send(lambda: (sc_pa.at[0], sfa_in.at[0], fas_sem.at[0], partner), same)
            send(lambda: (fa_out.at[0, other], fa_in.at[0], fa_sem.at[0], partner), same)

    relay_lower(2)
    relay_lower(1)
    relay_rows()
    relay_upper(0)
    relay_lower(3)
    relay_upper(1)
    relay_lower(0)

    value = column_sum(z)
    for i, d in ((0, 7), (1, 1)):
        wait(zd_in.at[i], zd_sem.at[i])
        value = value + decode(zd_in[i], lane(sz_in[d]))
    for i in (0, 1):
        wait(sz2_in.at[i], zsc2_sem.at[i])
        wait(z2_in.at[i], z2_sem.at[i])
        value = value + decode(z2_in[i], lane(sz2_in[i]))
    oq_ref[...] = value

    for parts, scales, psem, sem, half in ((fb_in, sfb_in, fb_sem, fbs_sem, high), (fa_in, sfa_in, fa_sem, fas_sem, low)):
        for e in range(4):

            def arrived(e=e, parts=parts, scales=scales, psem=psem, sem=sem):
                wait(scales.at[e], sem.at[e])
                wait(parts.at[e], psem.at[e])

            if e:
                arrived()
            else:
                pl.when(jnp.logical_not(same))(arrived)
        value = decode(parts[0], lane(scales[0]))
        for e in (1, 2, 3):
            value = value + decode(parts[e], lane(scales[e]))
        op_ref[half, :] = value

    settle()


N_SENDS = 81
Z_PEERS = (2, 6, 1, 7)
VMEM_LIMIT = 20 * 2**20


def local(queries, passages, query_lognorm, passage_lognorm, loss_cotangent):
    width = queries.shape[1]
    columns = passage_lognorm.shape[0]
    dma = pltpu.SemaphoreType.DMA
    vm = pltpu.VMEM
    scratch = [
        vm((16, ROWS, width), BF16), vm((16, ROWS, width), BF16), vm((ROWS, width), BF16), vm((16, 1, 128), F32), vm((1, columns), F32),
        vm((16 * ROWS, columns), BF16), vm((16 * ROWS, columns), BF16),
        vm((8, ROWS, width), F32), vm((4, 2, 2, ROWS, width), F32),
        vm((8, ROWS, width), F32), vm((8, ROWS, width), F32),
        vm((5, ROWS, width), BF16), vm((2, ROWS, width), BF16), vm((2, ROWS, width), BF16),
        vm((2, ROWS, width), BF16), vm((2, HALF, width), BF16), vm((2, ROWS, width), BF16),
        vm((2, 4, 2, HALF, width), BF16), vm((3, 4, 2, HALF, width), BF16),
        vm((3, 2, 2, HALF, width), BF16), vm((3, 2, 2, HALF, width), BF16),
        vm((4, 2, HALF, width), BF16), vm((4, HALF, width), BF16),
        vm((2, 2, HALF, width), BF16), vm((4, HALF, width), BF16),
        *[vm((n, 1, 128), F32) for n in (1, 1, 2, 1, 1, 1, 8, 2, 3, 3, 4, 4)],
        pltpu.SMEM((ROWS,), F32), dma((N_SENDS,)), dma((4,)), dma((16, 2)), dma((16,)), dma((16,)), dma((16,)), dma((1,)),
        dma((2,)), dma((1,)), dma((2,)), dma((2,)), dma((2,)), dma((2,)), dma((8,)), dma((2,)),
        dma((3, 4)), dma((3, 2)), dma((3,)), dma((3,)), dma((4,)), dma((4,)), dma((4,)), dma((4,)),
    ]
    out = jax.ShapeDtypeStruct(queries.shape, F32)
    vmem = pl.BlockSpec(memory_space=pltpu.VMEM)

    def kernel(*refs):
        body(width, *refs)

    sums = pl.pallas_call(
        kernel,
        out_shape=(out, out),
        in_specs=[pl.BlockSpec(memory_space=pltpu.HBM)] * 4,
        out_specs=[vmem] * 2,
        scratch_shapes=scratch,
        compiler_params=pltpu.CompilerParams(collective_id=0, has_side_effects=True, vmem_limit_bytes=VMEM_LIMIT),
    )(*[pltpu.with_memory_space_constraint(v, pltpu.HBM) for v in (queries, passages, query_lognorm, passage_lognorm)])

    sums = lax.optimization_barrier((sums[0], sums[1], loss_cotangent))
    factor = sums[2] * (1.0 / math.sqrt(width))
    return sums[0] * factor, sums[1] * factor


def solution(mesh):
    return jax.shard_map(
        local,
        mesh=mesh,
        in_specs=(
            P(("slab", "blk"), None),
            P(("blk", "slab"), None),
            P(("slab", "blk")),
            P("blk"),
            P(),
        ),
        out_specs=(P(("slab", "blk"), None), P(("blk", "slab"), None)),
        check_vma=False,
    )
```

```python
import math

import jax
import jax.numpy as jnp
from jax import lax
from jax.experimental import pallas as pl
from jax.experimental.pallas import tpu as pltpu
from jax.sharding import PartitionSpec as P

MESH = pl.DeviceIdType.MESH
F32, BF16 = jnp.float32, jnp.bfloat16
ROWS = 32
HALF = 16
BATCH = 8192
LOG2E = math.log2(math.e)
TOP = math.log(BATCH) + 3.5
BOUND = 512 * 6.0 * 2.0**-30
TINY = 1e-37


def encode(value, inverse):
    t = value * inverse
    u = t * jnp.abs(t)
    return (u * jnp.abs(u)).astype(BF16)


def decode(coded, scale):
    wide = coded.astype(F32)
    r = lax.rsqrt(jnp.maximum(jnp.abs(wide), TINY))
    return (wide * r) * (r * lax.rsqrt(r)) * scale


def body(
    width,
    q_in, p_in, qn_in, pn_in,
    oq_ref, op_ref,
    q_all, p_all, p_own, qn_all, pn_all,
    w_hi, w_lo, g_q, g_p, xq_out, xq_in,
    zs1, zs2, zd_in, zf_in, zh_in, z2_in,
    pa_out, pa_in, pb_out, pb_in,
    fa_out, fa_in, fb_out, fb_in,
    sc_me, sc_q, sc_qr, sc_pa, sc_pb, sx_in, sz_in, sz2_in, sy1_in, sx1_in, sfa_in, sfb_in,
    spare, qn_smem, ssem, lsem, q_sem, qn_sem, pa_sem, pb_sem, pn_sem,
    xq_sem, xs_sem, zd_sem, zr_sem, z2_sem, zsc_sem, zsc2_sem,
    ra_sem, rb_sem, ras_sem, rbs_sem, fa_sem, fb_sem, fas_sem, fbs_sem,
):
    slab, blk = lax.axis_index("slab"), lax.axis_index("blk")

    def ring(value, size):
        return [value] + [lax.rem(value + d, size) for d in range(1, size)]

    x, c = lax.div(slab, 4), lax.rem(slab, 2)
    yl = lax.rem(lax.div(slab, 2), 2)
    z, yh = lax.div(blk, 2), lax.rem(blk, 2)
    y = yh * 2 + yl
    xs, ys, zs = ring(x, 4), ring(y, 4), ring(z, 8)
    in_row, in_block = yl * 2, z * 2 + yh
    y_row = [(lax.rem(yy, 2) * 2, z * 2 + lax.div(yy, 2)) for yy in ys]
    other = 1 - c
    same = c == yh
    partner = (slab + 1 - 2 * c, blk)

    def at_x(d, cc):
        return (xs[d] * 4 + in_row + cc, in_block)

    def at_y(d, cc):
        return (x * 4 + y_row[d][0] + cc, y_row[d][1])

    def at_z(d):
        return (slab, zs[d] * 2 + yh)

    def at_owner(yy, cc):
        return (x * 4 + yy * 2 + cc, z * 2 + c)

    def halves_of(n):
        if n % 2 == 0:
            return q_all.at[pl.ds(0, n // 2)]
        return spare.at[pl.ds(0, n)]

    def rows_of(n):
        return qn_all.at[pl.ds(0, n)]

    def sums_of(n):
        return xq_in.at[pl.ds(0, n)]

    room = {halves_of: 32, rows_of: 16, sums_of: 8}
    groups = []

    def send(build, when=None, size=1, kind=halves_of):
        for group in groups:
            if group["when"] is when and group["kind"] is kind and group["size"] + size <= room[kind]:
                break
        else:
            group = {"when": when, "kind": kind, "size": 0, "index": len(groups)}
            groups.append(group)
        group["size"] += size
        index = group["index"]

        def go():
            src, dst, rsem, to = build()
            pltpu.make_async_remote_copy(
                src_ref=src, dst_ref=dst, send_sem=ssem.at[index], recv_sem=rsem, device_id=to, device_id_type=MESH
            ).start()

        if when is None:
            go()
        else:
            pl.when(when)(go)

    def row(build, when=None):
        send(build, when, 1, rows_of)

    def wait(what, rsem):
        pltpu.make_async_remote_copy(
            src_ref=what, dst_ref=what, send_sem=lsem.at[0], recv_sem=rsem, device_id=partner, device_id_type=MESH
        ).wait_recv()

    def settle():
        assert len(groups) <= N_SENDS
        for group in groups:

            def done(group=group):
                what = group["kind"](group["size"])
                pltpu.make_async_remote_copy(
                    src_ref=what,
                    dst_ref=what,
                    send_sem=ssem.at[group["index"]],
                    recv_sem=lsem.at[0],
                    device_id=partner,
                    device_id_type=MESH,
                ).wait_send()

            if group["when"] is None:
                done()
            else:
                pl.when(group["when"])(done)

    me_q = c * 8 + z
    low, high = pl.ds(0, HALF), pl.ds(HALF, HALF)
    halves = (low, high)
    norms = pltpu.make_async_copy(qn_in, qn_smem, lsem.at[2])
    local_q = pltpu.make_async_copy(q_in, q_all.at[me_q], lsem.at[1])
    local_p = pltpu.make_async_copy(p_in, p_own, lsem.at[3])
    local_p.start()
    local_q.start()
    norms.start()
    barrier = pltpu.get_barrier_semaphore()
    peers = [at_x(2, cc) for cc in (0, 1)] + [at_y(2, cc) for cc in (0, 1)]
    peers += [at_x(d, cc) for d in (1, 3) for cc in (0, 1)]
    peers += [at_y(d, cc) for d in (1, 3) for cc in (0, 1)]
    peers += [at_z(d) for d in Z_PEERS]
    peers += [partner]
    for peer in peers:
        pl.semaphore_signal(barrier, inc=1, device_id=peer, device_id_type=MESH)

    @pl.when(same)
    def _():
        pltpu.make_async_copy(p_in, p_all.at[slab], lsem.at[4]).start()
        pltpu.make_async_copy(pn_in, pn_all.at[0], lsem.at[5]).start()

    local_p.wait()
    local_q.wait()
    pl.semaphore_wait(barrier, len(peers))

    def own(half, rsem, to, when=None):
        send(lambda: (p_own.at[half], p_all.at[slab, half], rsem, to), when)

    def q_half(slot, h, rsem, to):
        send(lambda: (q_all.at[slot, halves[h]], q_all.at[slot, halves[h]], rsem, to))

    def q_block(slot, rsem, to):
        send(lambda: (q_all.at[slot], q_all.at[slot], rsem, to), None, 2)

    def n_send(slot, rsem, to):
        row(lambda: (qn_all.at[slot], qn_all.at[slot], rsem, to))

    apart = jnp.logical_not(same)
    own(low, pa_sem.at[0], partner, apart)
    own(high, pb_sem.at[yl], partner, apart)
    q_half(me_q, 0, q_sem.at[2], at_z(2))
    q_half(me_q, 1, q_sem.at[5], at_z(6))
    for d in (1, 3):
        own(low, pa_sem.at[4 - d], at_x(d, yh))
        own(high, pb_sem.at[yl], at_y(d, yh))
    q_half(me_q, 1, q_sem.at[3], at_z(2))
    q_half(me_q, 0, q_sem.at[4], at_z(6))
    q_block(me_q, q_sem.at[0], at_z(1))
    q_block(me_q, q_sem.at[1], at_z(7))
    own(low, pa_sem.at[2], at_x(2, yh))
    own(high, pb_sem.at[yl], at_y(2, yh))
    for d in (1, 3, 2):
        own(low, pa_sem.at[4], at_y(d, c), same)
        own(high, pb_sem.at[2], at_x(d, c), same)
    q_block(me_q, q_sem.at[9], partner)

    @pl.when(same)
    def _():
        copy = pltpu.make_async_remote_copy(
            src_ref=pn_in,
            dst_ref=pn_all.at[0],
            send_sem=lsem.at[6],
            recv_sem=pn_sem.at[0],
            device_id=at_y(2, c),
            device_id_type=MESH,
        )
        copy.start()

    norms.wait()
    lanes = lax.broadcasted_iota(jnp.int32, (1, 128), 1)
    line = jnp.zeros((1, 128), F32)
    for i in range(ROWS):
        line = jnp.where(lanes == i, qn_smem[i], line)
    qn_all[me_q] = line
    for i, to in ((2, at_z(2)), (3, at_z(6)), (0, at_z(1)), (1, at_z(7)), (7, partner)):
        n_send(me_q, qn_sem.at[i], to)

    def relay_a(e, ccs):
        first = xs[e] * 4 + in_row

        @pl.when(same)
        def _():
            wait(halves_of(len(ccs)), pa_sem.at[e])

        for cc in ccs:
            slot = first + cc
            for d in (1, 3, 2):
                send(
                    lambda slot=slot, d=d: (p_all.at[slot, low], p_all.at[slot, low], pa_sem.at[4], at_y(d, c)), same
                )

    def relay_b(yy, ccs, when=None):
        def arrive():
            wait(halves_of(len(ccs)), pb_sem.at[yy])

        if when is None:
            arrive()
        else:
            pl.when(when)(arrive)
        for cc in ccs:
            slot = x * 4 + yy * 2 + cc
            for d in (1, 3, 2):
                send(
                    lambda slot=slot, d=d: (p_all.at[slot, high], p_all.at[slot, high], pb_sem.at[2], at_x(d, c)), when
                )

    relay_a(0, (other,))
    relay_b(yl, (other,), same)
    relay_a(1, (0, 1))
    relay_a(3, (0, 1))
    relay_b(yl, (0, 1), apart)
    relay_b(1 - yl, (0, 1))
    slots = {k: (c * 8 + zs[8 - k], c * 8 + zs[k]) for k in (1, 2, 3)}
    left, right = slots[2]
    wait(halves_of(1), q_sem.at[2])
    q_half(left, 0, q_sem.at[8], at_z(2))
    q_half(left, 0, q_sem.at[6], at_z(1))
    q_half(left, 0, q_sem.at[9], partner)
    wait(halves_of(1), q_sem.at[5])
    q_half(right, 1, q_sem.at[8], at_z(6))
    q_half(right, 1, q_sem.at[7], at_z(7))
    q_half(right, 1, q_sem.at[9], partner)
    relay_a(2, (0, 1))
    wait(halves_of(1), q_sem.at[3])
    q_half(left, 1, q_sem.at[6], at_z(1))
    q_half(left, 1, q_sem.at[9], partner)
    wait(halves_of(1), q_sem.at[4])
    q_half(right, 0, q_sem.at[7], at_z(7))
    q_half(right, 0, q_sem.at[9], partner)
    wait(rows_of(1), qn_sem.at[2])
    n_send(left, qn_sem.at[6], at_z(2))
    n_send(left, qn_sem.at[4], at_z(1))
    n_send(left, qn_sem.at[7], partner)
    wait(rows_of(1), qn_sem.at[3])
    n_send(right, qn_sem.at[5], at_z(7))
    n_send(right, qn_sem.at[7], partner)
    for i, slot in ((0, slots[1][0]), (1, slots[1][1]), (6, slots[3][0]), (7, slots[3][1]), (8, c * 8 + zs[4])):
        wait(halves_of(2), q_sem.at[i])
        q_block(slot, q_sem.at[9], partner)
        n = i if i < 2 else i - 2
        wait(rows_of(1), qn_sem.at[n])
        n_send(slot, qn_sem.at[7], partner)

    @pl.when(same)
    def _():
        wait(halves_of(8), pa_sem.at[4])
        pltpu.make_async_copy(p_in, p_all.at[slab], lsem.at[4]).wait()
        pltpu.make_async_copy(pn_in, pn_all.at[0], lsem.at[5]).wait()
        pltpu.make_async_remote_copy(
            src_ref=pn_in,
            dst_ref=pn_all.at[0],
            send_sem=lsem.at[6],
            recv_sem=pn_sem.at[0],
            device_id=at_y(2, c),
            device_id_type=MESH,
        ).wait_send()

    @pl.when(apart)
    def _():
        wait(halves_of(16), pa_sem.at[4])
        wait(pn_all.at[0], pn_sem.at[0])

    wait(halves_of(12), pb_sem.at[2])
    wait(halves_of(16), q_sem.at[9])
    wait(rows_of(8), qn_sem.at[7])

    scale = 2.0 / math.sqrt(width)
    columns = pn_all.shape[1]
    b = jnp.exp(TOP - pn_all[...])
    a_t = jnp.exp(TOP - qn_all[...].reshape(16, 128)).T
    passages = p_all[...].reshape(columns, width)
    largest = jnp.zeros((8, 128), F32)
    column = lax.broadcasted_iota(jnp.int32, (ROWS, columns), 1) - lax.broadcasted_iota(jnp.int32, (ROWS, columns), 0)
    for chunk in range(4):
        rows = q_all[pl.ds(chunk * 4, 4)].reshape(4 * ROWS, width)
        scores = lax.dot_general(rows, passages, (((1,), (1,)), ((), ())), preferred_element_type=F32)
        terms = jnp.exp2(scores * (scale * LOG2E) - TOP * LOG2E)
        for k in range(4):
            slot = chunk * 4 + k
            first = ((x * 4 + yl * 2 + slot // 8) * 16 + (slot % 8) * 2 + yh) * ROWS - (z * 2 + c) * columns
            here = slice(k * ROWS, (k + 1) * ROWS)
            weights = terms[here] * (a_t[:ROWS, slot : slot + 1] + b) - jnp.where(column == first, 2.0, 0.0)
            top = weights.astype(BF16)
            at = pl.ds(slot * ROWS, ROWS)
            w_hi[at, :] = top
            w_lo[at, :] = (weights - top.astype(F32)).astype(BF16)
            size = jnp.abs(weights)
            size = jnp.maximum(size[:HALF], size[HALF:])
            size = jnp.maximum(size[:8], size[8:])
            for j in range(columns // 128):
                largest = jnp.maximum(largest, size[:, j * 128 : (j + 1) * 128])
    mine = jnp.maximum(jnp.max(largest, axis=(0, 1), keepdims=True), 1e-30) * BOUND
    mine = jnp.broadcast_to(mine, (1, 128))
    sc_me[0] = mine
    row_of = [2 * c + yy for yy in (0, 1)]
    far_row = [row != y for row in row_of]
    back_a = [lax.rem(y - row + 3 + 4, 4) for row in row_of]
    back_b = [lax.rem(y - row + 4, 4) for row in row_of]
    row(lambda: (sc_me.at[0], sx_in.at[0], xs_sem.at[0], partner))
    for d in (2, 1, 3):
        row(lambda d=d: (sc_me.at[0], sx1_in.at[3 - d], rbs_sem.at[0], at_x(d, c)))
    for yy in (0, 1):
        row(
            lambda yy=yy: (sc_me.at[0], sy1_in.at[back_a[yy]], ras_sem.at[0], at_owner(yy, c)),
            far_row[yy],
        )

    def lane(row):
        return row[:, :1]

    inverse = lane(1.0 / mine)

    for chunk in range(2):
        at = pl.ds(pl.multiple_of(other * 8 * ROWS + chunk * 4 * ROWS, 4 * ROWS), 4 * ROWS)
        part = jnp.dot(w_hi[at, :], passages, preferred_element_type=F32)
        part += jnp.dot(w_lo[at, :], passages, preferred_element_type=F32)
        to = pl.ds(chunk * 4, 4)
        xq_out[to] = part.reshape(4, ROWS, width)
        send(lambda to=to: (xq_out.at[to], xq_in.at[to], xq_sem.at[0], partner), None, 4, sums_of)
    for chunk in range(2):
        at = pl.ds(pl.multiple_of(c * 8 * ROWS + chunk * 4 * ROWS, 4 * ROWS), 4 * ROWS)
        part = jnp.dot(w_hi[at, :], passages, preferred_element_type=F32)
        part += jnp.dot(w_lo[at, :], passages, preferred_element_type=F32)
        g_q[pl.ds(chunk * 4, 4)] = part.reshape(4, ROWS, width)

    queries = q_all[...].reshape(16 * ROWS, width)
    across = (((0,), (0,)), ((), ()))

    def passage_chunk(d):
        xm = xs[d]
        at = pl.ds(pl.multiple_of(xm * 4 * ROWS, 4 * ROWS), 4 * ROWS)
        part = lax.dot_general(w_hi[:, at], queries, across, preferred_element_type=F32)
        part += lax.dot_general(w_lo[:, at], queries, across, preferred_element_type=F32)
        part = part.reshape(2, 2, ROWS, width)
        g_p[xm] = part
        for yy in (0, 1):
            coded = encode(part[yy], inverse)
            pa_out[yy, xm] = coded[:, :HALF]
            if d:
                pb_out[3 - d, yy] = coded[:, HALF:]
                send(lambda yy=yy: (pb_out.at[3 - d, yy], pb_in.at[3 - d, yy], rb_sem.at[yy], at_x(d, c)), None, 2)
            send(
                lambda yy=yy: (pa_out.at[yy, xm], pa_in.at[back_a[yy], xm], ra_sem.at[xm], at_owner(yy, c)),
                far_row[yy],
                2,
            )

    passage_chunk(2)

    wait(rows_of(1), xs_sem.at[0])
    both = mine + sx_in[0]
    sc_q[0] = both
    wait(sums_of(8), xq_sem.at[0])
    for d in (1, 2, 6, 7):
        row(lambda d=d: (sc_q.at[0], sz_in.at[8 - d], zsc_sem.at[0], at_z(d)))
    inverse_q = lane(1.0 / both)

    def column_sum(zz):
        return g_q[zz] + xq_in[zz]

    far = encode(column_sum(zs[4]), inverse_q)
    zs1[4, low] = far[:HALF]
    zs1[4, high] = far[HALF:]
    for i, d in enumerate((5, 3)):
        zs1[i] = encode(column_sum(zs[d]), inverse_q)
    for i, d in enumerate((1, 7)):
        zs1[2 + i] = encode(column_sum(zs[d]), inverse_q)
    send(lambda: (zs1.at[4, low], zh_in.at[0], zr_sem.at[0], at_z(6)))
    send(lambda: (zs1.at[4, high], zh_in.at[1], zr_sem.at[1], at_z(2)))
    send(lambda: (zs1.at[0], zf_in.at[0], zr_sem.at[0], at_z(7)), None, 2)
    send(lambda: (zs1.at[1], zf_in.at[1], zr_sem.at[1], at_z(1)), None, 2)
    send(lambda: (zs1.at[2], zd_in.at[0], zd_sem.at[0], at_z(1)), None, 2)
    send(lambda: (zs1.at[3], zd_in.at[1], zd_sem.at[0], at_z(7)), None, 2)

    for d in (1, 3, 0):
        passage_chunk(d)

    def relay_rows():
        wait(rows_of(4), zsc_sem.at[0])
        for i in (0, 1):
            near, far_ = (1, 2) if i == 0 else (7, 6)
            to = at_z(6 if i == 0 else 2)
            wait(halves_of(3), zr_sem.at[i])
            total = both + sz_in[near] + sz_in[far_]
            sc_qr[i] = total
            value = column_sum(zs[6 if i == 0 else 2]) + decode(zf_in[i], lane(sz_in[near]))
            extra = decode(zh_in[i], lane(sz_in[far_]))
            inv = lane(1.0 / total)
            first_half, second_half = value[:HALF], value[HALF:]
            if i == 0:
                first_half = first_half + extra
            else:
                second_half = second_half + extra
            zs2[i, low] = encode(first_half, inv)
            zs2[i, high] = encode(second_half, inv)
            row(lambda i=i, to=to: (sc_qr.at[i], sz2_in.at[i], zsc2_sem.at[0], to))
            send(lambda i=i, to=to: (zs2.at[i], z2_in.at[i], z2_sem.at[0], to), None, 2)

    total_b = []

    def relay_upper(yy):
        if not total_b:
            wait(rows_of(3), rbs_sem.at[0])
            total_b.append(mine + sx1_in[0] + sx1_in[1] + sx1_in[2])
            sc_pb[0] = total_b[0]
        inv_b = lane(1.0 / total_b[0])
        wait(halves_of(6), rb_sem.at[yy])
        for cc in (0, 1):
            value = g_p[x, yy, cc, HALF:]
            for d in (2, 1, 3):
                value = value + decode(pb_in[d - 1, yy, cc], lane(sx1_in[d - 1]))
            fb_out[yy, cc] = encode(value, inv_b)
        for cc in (0, 1):
            mine_too = jnp.logical_and(jnp.logical_not(far_row[yy]), c == cc)

            @pl.when(mine_too)
            def _(cc=cc):
                fb_in[0] = fb_out[yy, cc]
                sfb_in[0] = total_b[0]

            away = jnp.logical_not(mine_too)
            back, to = back_b[yy], at_owner(yy, cc)
            row(lambda back=back, to=to: (sc_pb.at[0], sfb_in.at[back], fbs_sem.at[0], to), away)
            send(lambda cc=cc, back=back, to=to: (fb_out.at[yy, cc], fb_in.at[back], fb_sem.at[0], to), away)

    def relay_lower(e):
        xm = xs[e]

        @pl.when(same)
        def _():
            if e == 2:
                wait(rows_of(3), ras_sem.at[0])
                sc_pa[0] = mine + sy1_in[0] + sy1_in[1] + sy1_in[2]
            inv_a = lane(1.0 / sc_pa[0])
            wait(halves_of(6), ra_sem.at[xm])
            for cc in (0, 1):
                value = g_p[xm, yl, cc, :HALF]
                for d in (1, 2, 3):
                    value = value + decode(pa_in[d - 1, xm, cc], lane(sy1_in[d - 1]))
                fa_out[e, cc] = encode(value, inv_a)
            if e == 0:
                fa_in[0] = fa_out[0, c]
                sfa_in[0] = sc_pa[0]

        if e:
            back = 4 - e
            for cc in (0, 1):
                row(lambda cc=cc: (sc_pa.at[0], sfa_in.at[back], fas_sem.at[0], at_x(e, cc)), same)
                send(lambda cc=cc: (fa_out.at[e, cc], fa_in.at[back], fa_sem.at[0], at_x(e, cc)), same)
        else:
            row(lambda: (sc_pa.at[0], sfa_in.at[0], fas_sem.at[0], partner), same)
            send(lambda: (fa_out.at[0, other], fa_in.at[0], fa_sem.at[0], partner), same)

    relay_lower(2)
    relay_lower(1)
    relay_rows()
    relay_upper(0)
    relay_lower(3)
    relay_upper(1)
    relay_lower(0)

    value = column_sum(z)
    wait(halves_of(4), zd_sem.at[0])
    for i, d in ((0, 7), (1, 1)):
        value = value + decode(zd_in[i], lane(sz_in[d]))
    wait(rows_of(2), zsc2_sem.at[0])
    wait(halves_of(4), z2_sem.at[0])
    for i in (0, 1):
        value = value + decode(z2_in[i], lane(sz2_in[i]))
    oq_ref[...] = value

    for parts, scales, psem, sem, half in ((fb_in, sfb_in, fb_sem, fbs_sem, high), (fa_in, sfa_in, fa_sem, fas_sem, low)):
        for n, when in ((3, same), (4, apart)):

            @pl.when(when)
            def _(n=n, psem=psem, sem=sem):
                wait(rows_of(n), sem.at[0])
                wait(halves_of(n), psem.at[0])

        value = decode(parts[0], lane(scales[0]))
        for e in (1, 2, 3):
            value = value + decode(parts[e], lane(scales[e]))
        op_ref[half, :] = value

    settle()


N_SENDS = 28
Z_PEERS = (2, 6, 1, 7)
VMEM_LIMIT = 20 * 2**20


def local(queries, passages, query_lognorm, passage_lognorm, loss_cotangent):
    width = queries.shape[1]
    columns = passage_lognorm.shape[0]
    dma = pltpu.SemaphoreType.DMA
    vm = pltpu.VMEM
    scratch = [
        vm((16, ROWS, width), BF16), vm((16, ROWS, width), BF16), vm((ROWS, width), BF16), vm((16, 1, 128), F32), vm((1, columns), F32),
        vm((16 * ROWS, columns), BF16), vm((16 * ROWS, columns), BF16),
        vm((8, ROWS, width), F32), vm((4, 2, 2, ROWS, width), F32),
        vm((8, ROWS, width), F32), vm((8, ROWS, width), F32),
        vm((5, ROWS, width), BF16), vm((2, ROWS, width), BF16), vm((2, ROWS, width), BF16),
        vm((2, ROWS, width), BF16), vm((2, HALF, width), BF16), vm((2, ROWS, width), BF16),
        vm((2, 4, 2, HALF, width), BF16), vm((3, 4, 2, HALF, width), BF16),
        vm((3, 2, 2, HALF, width), BF16), vm((3, 2, 2, HALF, width), BF16),
        vm((4, 2, HALF, width), BF16), vm((4, HALF, width), BF16),
        vm((2, 2, HALF, width), BF16), vm((4, HALF, width), BF16),
        *[vm((n, 1, 128), F32) for n in (1, 1, 2, 1, 1, 1, 8, 2, 3, 3, 4, 4)],
        vm((8, HALF, width), BF16), pltpu.SMEM((ROWS,), F32), dma((N_SENDS,)), dma((7,)), dma((10,)), dma((8,)), dma((5,)), dma((3,)), dma((1,)),
        *[dma((n,)) for n in (1, 1, 1, 2, 1, 1, 1, 4, 2, 1, 1, 1, 1, 1, 1)],
    ]
    out = jax.ShapeDtypeStruct(queries.shape, F32)
    vmem = pl.BlockSpec(memory_space=pltpu.VMEM)

    def kernel(*refs):
        body(width, *refs)

    sums = pl.pallas_call(
        kernel,
        out_shape=(out, out),
        in_specs=[pl.BlockSpec(memory_space=pltpu.HBM)] * 4,
        out_specs=[vmem] * 2,
        scratch_shapes=scratch,
        compiler_params=pltpu.CompilerParams(collective_id=0, has_side_effects=True, vmem_limit_bytes=VMEM_LIMIT),
    )(*[pltpu.with_memory_space_constraint(v, pltpu.HBM) for v in (queries, passages, query_lognorm, passage_lognorm)])

    sums = lax.optimization_barrier((sums[0], sums[1], loss_cotangent))
    factor = sums[2] * (1.0 / math.sqrt(width))
    return sums[0] * factor, sums[1] * factor


def solution(mesh):
    return jax.shard_map(
        local,
        mesh=mesh,
        in_specs=(
            P(("slab", "blk"), None),
            P(("blk", "slab"), None),
            P(("slab", "blk")),
            P("blk"),
            P(),
        ),
        out_specs=(P(("slab", "blk"), None), P(("blk", "slab"), None)),
        check_vma=False,
    )
```

```python
import math

import jax
import jax.numpy as jnp
from jax import lax
from jax.experimental import pallas as pl
from jax.experimental.pallas import tpu as pltpu
from jax.sharding import PartitionSpec as P

MESH = pl.DeviceIdType.MESH
F32, BF16 = jnp.float32, jnp.bfloat16
ROWS = 32
HALF = 16
BATCH = 8192
LOG2E = math.log2(math.e)
TOP = math.log(BATCH) + 3.5
BOUND = 512 * 6.0 * 2.0**-30
TINY = 1e-37


def encode(value, inverse):
    t = value * inverse
    u = t * jnp.abs(t)
    return (u * jnp.abs(u)).astype(BF16)


def decode(coded, scale):
    wide = coded.astype(F32)
    r = lax.rsqrt(jnp.maximum(jnp.abs(wide), TINY))
    return (wide * r) * (r * lax.rsqrt(r)) * scale


def body(
    width,
    q_in, p_in, qn_in, pn_in,
    oq_ref, op_ref,
    q_all, p_all, p_own, qn_all, pn_all,
    w_hi, w_lo, g_q, g_p, xq_out, xq_in,
    zs1, zs2, zd_in, zf_in, zh_in, z2_in,
    pa_out, pa_in, pb_out, pb_in,
    fa_out, fa_in, fb_out, fb_in,
    sc_me, sc_q, sc_qr, sc_pa, sc_pb, sx_in, sz_in, sz2_in, sy1_in, sx1_in, sfa_in, sfb_in,
    spare, qn_smem, ssem, lsem, q_sem, qn_sem, pa_sem, pb_sem, pn_sem,
    xq_sem, xs_sem, zd_sem, zr_sem, z2_sem, zsc_sem, zsc2_sem,
    ra_sem, rb_sem, ras_sem, rbs_sem, fa_sem, fb_sem, fas_sem, fbs_sem,
):
    slab, blk = lax.axis_index("slab"), lax.axis_index("blk")

    def ring(value, size):
        return [value] + [lax.rem(value + d, size) for d in range(1, size)]

    x, c = lax.div(slab, 4), lax.rem(slab, 2)
    yl = lax.rem(lax.div(slab, 2), 2)
    z, yh = lax.div(blk, 2), lax.rem(blk, 2)
    y = yh * 2 + yl
    xs, ys, zs = ring(x, 4), ring(y, 4), ring(z, 8)
    in_row, in_block = yl * 2, z * 2 + yh
    y_row = [(lax.rem(yy, 2) * 2, z * 2 + lax.div(yy, 2)) for yy in ys]
    other = 1 - c
    same = c == yh
    partner = (slab + 1 - 2 * c, blk)

    def at_x(d, cc):
        return (xs[d] * 4 + in_row + cc, in_block)

    def at_y(d, cc):
        return (x * 4 + y_row[d][0] + cc, y_row[d][1])

    def at_z(d):
        return (slab, zs[d] * 2 + yh)

    def at_owner(yy, cc):
        return (x * 4 + yy * 2 + cc, z * 2 + c)

    def halves_of(n):
        if n % 2 == 0:
            return q_all.at[pl.ds(0, n // 2)]
        return spare.at[pl.ds(0, n)]

    def rows_of(n):
        return qn_all.at[pl.ds(0, n)]

    def sums_of(n):
        return xq_in.at[pl.ds(0, n)]

    room = {halves_of: 32, rows_of: 16, sums_of: 8}
    groups = []

    def send(build, when=None, size=1, kind=halves_of):
        for group in groups:
            if group["when"] is when and group["kind"] is kind and group["size"] + size <= room[kind]:
                break
        else:
            group = {"when": when, "kind": kind, "size": 0, "index": len(groups)}
            groups.append(group)
        group["size"] += size
        index = group["index"]

        def go():
            src, dst, rsem, to = build()
            pltpu.make_async_remote_copy(
                src_ref=src, dst_ref=dst, send_sem=ssem.at[index], recv_sem=rsem, device_id=to, device_id_type=MESH
            ).start()

        if when is None:
            go()
        else:
            pl.when(when)(go)

    def row(build, when=None):
        send(build, when, 1, rows_of)

    def wait(what, rsem):
        pltpu.make_async_remote_copy(
            src_ref=what, dst_ref=what, send_sem=lsem.at[0], recv_sem=rsem, device_id=partner, device_id_type=MESH
        ).wait_recv()

    def settle():
        assert len(groups) <= N_SENDS
        for group in groups:

            def done(group=group):
                what = group["kind"](group["size"])
                pltpu.make_async_remote_copy(
                    src_ref=what,
                    dst_ref=what,
                    send_sem=ssem.at[group["index"]],
                    recv_sem=lsem.at[0],
                    device_id=partner,
                    device_id_type=MESH,
                ).wait_send()

            if group["when"] is None:
                done()
            else:
                pl.when(group["when"])(done)

    me_q = c * 8 + z
    low, high = pl.ds(0, HALF), pl.ds(HALF, HALF)
    halves = (low, high)
    norms = pltpu.make_async_copy(qn_in, qn_smem, lsem.at[2])
    local_q = pltpu.make_async_copy(q_in, q_all.at[me_q], lsem.at[1])
    local_p = pltpu.make_async_copy(p_in, p_own, lsem.at[3])
    local_p.start()
    local_q.start()
    norms.start()
    barrier = pltpu.get_barrier_semaphore()
    peers = [at_x(2, cc) for cc in (0, 1)] + [at_y(2, cc) for cc in (0, 1)]
    peers += [at_x(d, cc) for d in (1, 3) for cc in (0, 1)]
    peers += [at_y(d, cc) for d in (1, 3) for cc in (0, 1)]
    peers += [at_z(d) for d in Z_PEERS]
    peers += [partner]
    for peer in peers:
        pl.semaphore_signal(barrier, inc=1, device_id=peer, device_id_type=MESH)

    @pl.when(same)
    def _():
        pltpu.make_async_copy(p_in, p_all.at[slab], lsem.at[4]).start()
        pltpu.make_async_copy(pn_in, pn_all.at[0], lsem.at[5]).start()

    local_p.wait()
    local_q.wait()
    pl.semaphore_wait(barrier, len(peers))

    def own(half, rsem, to, when=None):
        send(lambda: (p_own.at[half], p_all.at[slab, half], rsem, to), when)

    def q_half(slot, h, rsem, to):
        send(lambda: (q_all.at[slot, halves[h]], q_all.at[slot, halves[h]], rsem, to))

    def q_block(slot, rsem, to):
        send(lambda: (q_all.at[slot], q_all.at[slot], rsem, to), None, 2)

    def n_send(slot, rsem, to):
        row(lambda: (qn_all.at[slot], qn_all.at[slot], rsem, to))

    apart = jnp.logical_not(same)
    own(low, pa_sem.at[0], partner, apart)
    own(high, pb_sem.at[yl], partner, apart)
    q_half(me_q, 0, q_sem.at[2], at_z(2))
    q_half(me_q, 1, q_sem.at[5], at_z(6))
    for d in (1, 3):
        own(low, pa_sem.at[4 - d], at_x(d, yh))
        own(high, pb_sem.at[yl], at_y(d, yh))
    q_half(me_q, 1, q_sem.at[3], at_z(2))
    q_half(me_q, 0, q_sem.at[4], at_z(6))
    q_block(me_q, q_sem.at[0], at_z(1))
    q_block(me_q, q_sem.at[1], at_z(7))
    own(low, pa_sem.at[2], at_x(2, yh))
    own(high, pb_sem.at[yl], at_y(2, yh))
    for d in (1, 3, 2):
        own(low, pa_sem.at[4], at_y(d, c), same)
        own(high, pb_sem.at[2], at_x(d, c), same)
    q_block(me_q, q_sem.at[9], partner)

    @pl.when(same)
    def _():
        copy = pltpu.make_async_remote_copy(
            src_ref=pn_in,
            dst_ref=pn_all.at[0],
            send_sem=lsem.at[6],
            recv_sem=pn_sem.at[0],
            device_id=at_y(2, c),
            device_id_type=MESH,
        )
        copy.start()

    norms.wait()
    lanes = lax.broadcasted_iota(jnp.int32, (1, 128), 1)
    line = jnp.zeros((1, 128), F32)
    for i in range(ROWS):
        line = jnp.where(lanes == i, qn_smem[i], line)
    qn_all[me_q] = line
    for i, to in ((2, at_z(2)), (3, at_z(6)), (0, at_z(1)), (1, at_z(7)), (7, partner)):
        n_send(me_q, qn_sem.at[i], to)

    def relay_a(e, ccs):
        first = xs[e] * 4 + in_row

        @pl.when(same)
        def _():
            wait(halves_of(len(ccs)), pa_sem.at[e])

        for cc in ccs:
            slot = first + cc
            for d in (1, 3, 2):
                send(
                    lambda slot=slot, d=d: (p_all.at[slot, low], p_all.at[slot, low], pa_sem.at[4], at_y(d, c)), same
                )

    def relay_b(yy, ccs, when=None):
        def arrive():
            wait(halves_of(len(ccs)), pb_sem.at[yy])

        if when is None:
            arrive()
        else:
            pl.when(when)(arrive)
        for cc in ccs:
            slot = x * 4 + yy * 2 + cc
            for d in (1, 3, 2):
                send(
                    lambda slot=slot, d=d: (p_all.at[slot, high], p_all.at[slot, high], pb_sem.at[2], at_x(d, c)), when
                )

    relay_a(0, (other,))
    relay_b(yl, (other,), same)
    relay_a(1, (0, 1))
    relay_a(3, (0, 1))
    relay_b(yl, (0, 1), apart)
    relay_b(1 - yl, (0, 1))
    slots = {k: (c * 8 + zs[8 - k], c * 8 + zs[k]) for k in (1, 2, 3)}
    left, right = slots[2]
    wait(halves_of(1), q_sem.at[2])
    q_half(left, 0, q_sem.at[8], at_z(2))
    q_half(left, 0, q_sem.at[6], at_z(1))
    q_half(left, 0, q_sem.at[9], partner)
    wait(halves_of(1), q_sem.at[5])
    q_half(right, 1, q_sem.at[8], at_z(6))
    q_half(right, 1, q_sem.at[7], at_z(7))
    q_half(right, 1, q_sem.at[9], partner)
    relay_a(2, (0, 1))
    wait(halves_of(1), q_sem.at[3])
    q_half(left, 1, q_sem.at[6], at_z(1))
    q_half(left, 1, q_sem.at[9], partner)
    wait(halves_of(1), q_sem.at[4])
    q_half(right, 0, q_sem.at[7], at_z(7))
    q_half(right, 0, q_sem.at[9], partner)
    wait(rows_of(1), qn_sem.at[2])
    n_send(left, qn_sem.at[6], at_z(2))
    n_send(left, qn_sem.at[4], at_z(1))
    n_send(left, qn_sem.at[7], partner)
    wait(rows_of(1), qn_sem.at[3])
    n_send(right, qn_sem.at[5], at_z(7))
    n_send(right, qn_sem.at[7], partner)
    for i, slot in ((0, slots[1][0]), (1, slots[1][1]), (6, slots[3][0]), (7, slots[3][1]), (8, c * 8 + zs[4])):
        wait(halves_of(2), q_sem.at[i])
        q_block(slot, q_sem.at[9], partner)
        n = i if i < 2 else i - 2
        wait(rows_of(1), qn_sem.at[n])
        n_send(slot, qn_sem.at[7], partner)

    @pl.when(same)
    def _():
        wait(halves_of(8), pa_sem.at[4])
        pltpu.make_async_copy(p_in, p_all.at[slab], lsem.at[4]).wait()
        pltpu.make_async_copy(pn_in, pn_all.at[0], lsem.at[5]).wait()
        pltpu.make_async_remote_copy(
            src_ref=pn_in,
            dst_ref=pn_all.at[0],
            send_sem=lsem.at[6],
            recv_sem=pn_sem.at[0],
            device_id=at_y(2, c),
            device_id_type=MESH,
        ).wait_send()

    @pl.when(apart)
    def _():
        wait(halves_of(16), pa_sem.at[4])
        wait(pn_all.at[0], pn_sem.at[0])

    wait(halves_of(12), pb_sem.at[2])
    wait(halves_of(16), q_sem.at[9])
    wait(rows_of(8), qn_sem.at[7])

    scale = 2.0 / math.sqrt(width)
    columns = pn_all.shape[1]
    b = jnp.exp(TOP - pn_all[...])
    a_t = jnp.exp(TOP - qn_all[...].reshape(16, 128)).T
    passages = p_all[...].reshape(columns, width)
    largest = jnp.zeros((8, 128), F32)
    column = lax.broadcasted_iota(jnp.int32, (ROWS, columns), 1) - lax.broadcasted_iota(jnp.int32, (ROWS, columns), 0)
    for chunk in range(4):
        rows = q_all[pl.ds(chunk * 4, 4)].reshape(4 * ROWS, width)
        scores = lax.dot_general(rows, passages, (((1,), (1,)), ((), ())), preferred_element_type=F32)
        terms = jnp.exp2(scores * (scale * LOG2E) - TOP * LOG2E)
        for k in range(4):
            slot = chunk * 4 + k
            first = ((x * 4 + yl * 2 + slot // 8) * 16 + (slot % 8) * 2 + yh) * ROWS - (z * 2 + c) * columns
            here = slice(k * ROWS, (k + 1) * ROWS)
            weights = terms[here] * (a_t[:ROWS, slot : slot + 1] + b) - jnp.where(column == first, 2.0, 0.0)
            top = weights.astype(BF16)
            at = pl.ds(slot * ROWS, ROWS)
            w_hi[at, :] = top
            w_lo[at, :] = (weights - top.astype(F32)).astype(BF16)
            size = jnp.abs(weights)
            size = jnp.maximum(size[:HALF], size[HALF:])
            size = jnp.maximum(size[:8], size[8:])
            for j in range(columns // 128):
                largest = jnp.maximum(largest, size[:, j * 128 : (j + 1) * 128])
    mine = jnp.maximum(jnp.max(largest, axis=(0, 1), keepdims=True), 1e-30) * BOUND
    mine = jnp.broadcast_to(mine, (1, 128))
    sc_me[0] = mine
    row_of = [2 * c + yy for yy in (0, 1)]
    far_row = [row != y for row in row_of]
    back_a = [lax.rem(y - row + 3 + 4, 4) for row in row_of]
    back_b = [lax.rem(y - row + 4, 4) for row in row_of]
    row(lambda: (sc_me.at[0], sx_in.at[0], xs_sem.at[0], partner))
    for d in (2, 1, 3):
        row(lambda d=d: (sc_me.at[0], sx1_in.at[3 - d], rbs_sem.at[0], at_x(d, c)))
    for yy in (0, 1):
        row(
            lambda yy=yy: (sc_me.at[0], sy1_in.at[back_a[yy]], ras_sem.at[0], at_owner(yy, c)),
            far_row[yy],
        )

    def lane(row):
        return row[:, :1]

    inverse = lane(1.0 / mine)

    for chunk in range(2):
        at = pl.ds(pl.multiple_of(other * 8 * ROWS + chunk * 4 * ROWS, 4 * ROWS), 4 * ROWS)
        part = jnp.dot(w_hi[at, :], passages, preferred_element_type=F32)
        part += jnp.dot(w_lo[at, :], passages, preferred_element_type=F32)
        to = pl.ds(chunk * 4, 4)
        xq_out[to] = part.reshape(4, ROWS, width)
        send(lambda to=to: (xq_out.at[to], xq_in.at[to], xq_sem.at[0], partner), None, 4, sums_of)
    for chunk in range(2):
        at = pl.ds(pl.multiple_of(c * 8 * ROWS + chunk * 4 * ROWS, 4 * ROWS), 4 * ROWS)
        part = jnp.dot(w_hi[at, :], passages, preferred_element_type=F32)
        part += jnp.dot(w_lo[at, :], passages, preferred_element_type=F32)
        g_q[pl.ds(chunk * 4, 4)] = part.reshape(4, ROWS, width)

    queries = q_all[...].reshape(16 * ROWS, width)
    across = (((0,), (0,)), ((), ()))

    def passage_chunk(d):
        xm = xs[d]
        at = pl.ds(pl.multiple_of(xm * 4 * ROWS, 4 * ROWS), 4 * ROWS)
        part = lax.dot_general(w_hi[:, at], queries, across, preferred_element_type=F32)
        part += lax.dot_general(w_lo[:, at], queries, across, preferred_element_type=F32)
        part = part.reshape(2, 2, ROWS, width)
        g_p[xm] = part
        for yy in (0, 1):
            coded = encode(part[yy], inverse)
            pa_out[yy, xm] = coded[:, :HALF]
            if d:
                pb_out[3 - d, yy] = coded[:, HALF:]
                send(lambda yy=yy: (pb_out.at[3 - d, yy], pb_in.at[3 - d, yy], rb_sem.at[yy], at_x(d, c)), None, 2)
            send(
                lambda yy=yy: (pa_out.at[yy, xm], pa_in.at[back_a[yy], xm], ra_sem.at[xm], at_owner(yy, c)),
                far_row[yy],
                2,
            )

    passage_chunk(2)
    passage_chunk(1)

    wait(rows_of(1), xs_sem.at[0])
    both = mine + sx_in[0]
    sc_q[0] = both
    wait(sums_of(8), xq_sem.at[0])
    for d in (1, 2, 6, 7):
        row(lambda d=d: (sc_q.at[0], sz_in.at[8 - d], zsc_sem.at[0], at_z(d)))
    inverse_q = lane(1.0 / both)

    def column_sum(zz):
        return g_q[zz] + xq_in[zz]

    far = encode(column_sum(zs[4]), inverse_q)
    zs1[4, low] = far[:HALF]
    zs1[4, high] = far[HALF:]
    for i, d in enumerate((5, 3)):
        zs1[i] = encode(column_sum(zs[d]), inverse_q)
    for i, d in enumerate((1, 7)):
        zs1[2 + i] = encode(column_sum(zs[d]), inverse_q)
    send(lambda: (zs1.at[4, low], zh_in.at[0], zr_sem.at[0], at_z(6)))
    send(lambda: (zs1.at[4, high], zh_in.at[1], zr_sem.at[1], at_z(2)))
    send(lambda: (zs1.at[0], zf_in.at[0], zr_sem.at[0], at_z(7)), None, 2)
    send(lambda: (zs1.at[1], zf_in.at[1], zr_sem.at[1], at_z(1)), None, 2)
    send(lambda: (zs1.at[2], zd_in.at[0], zd_sem.at[0], at_z(1)), None, 2)
    send(lambda: (zs1.at[3], zd_in.at[1], zd_sem.at[0], at_z(7)), None, 2)

    for d in (3, 0):
        passage_chunk(d)

    def relay_rows():
        wait(rows_of(4), zsc_sem.at[0])
        for i in (0, 1):
            near, far_ = (1, 2) if i == 0 else (7, 6)
            to = at_z(6 if i == 0 else 2)
            wait(halves_of(3), zr_sem.at[i])
            total = both + sz_in[near] + sz_in[far_]
            sc_qr[i] = total
            value = column_sum(zs[6 if i == 0 else 2]) + decode(zf_in[i], lane(sz_in[near]))
            extra = decode(zh_in[i], lane(sz_in[far_]))
            inv = lane(1.0 / total)
            first_half, second_half = value[:HALF], value[HALF:]
            if i == 0:
                first_half = first_half + extra
            else:
                second_half = second_half + extra
            zs2[i, low] = encode(first_half, inv)
            zs2[i, high] = encode(second_half, inv)
            row(lambda i=i, to=to: (sc_qr.at[i], sz2_in.at[i], zsc2_sem.at[0], to))
            send(lambda i=i, to=to: (zs2.at[i], z2_in.at[i], z2_sem.at[0], to), None, 2)

    total_b = []

    def relay_upper(yy):
        if not total_b:
            wait(rows_of(3), rbs_sem.at[0])
            total_b.append(mine + sx1_in[0] + sx1_in[1] + sx1_in[2])
            sc_pb[0] = total_b[0]
        inv_b = lane(1.0 / total_b[0])
        wait(halves_of(6), rb_sem.at[yy])
        for cc in (0, 1):
            value = g_p[x, yy, cc, HALF:]
            for d in (2, 1, 3):
                value = value + decode(pb_in[d - 1, yy, cc], lane(sx1_in[d - 1]))
            fb_out[yy, cc] = encode(value, inv_b)
        for cc in (0, 1):
            mine_too = jnp.logical_and(jnp.logical_not(far_row[yy]), c == cc)

            @pl.when(mine_too)
            def _(cc=cc):
                fb_in[0] = fb_out[yy, cc]
                sfb_in[0] = total_b[0]

            away = jnp.logical_not(mine_too)
            back, to = back_b[yy], at_owner(yy, cc)
            row(lambda back=back, to=to: (sc_pb.at[0], sfb_in.at[back], fbs_sem.at[0], to), away)
            send(lambda cc=cc, back=back, to=to: (fb_out.at[yy, cc], fb_in.at[back], fb_sem.at[0], to), away)

    def relay_lower(e):
        xm = xs[e]

        @pl.when(same)
        def _():
            if e == 2:
                wait(rows_of(3), ras_sem.at[0])
                sc_pa[0] = mine + sy1_in[0] + sy1_in[1] + sy1_in[2]
            inv_a = lane(1.0 / sc_pa[0])
            wait(halves_of(6), ra_sem.at[xm])
            for cc in (0, 1):
                value = g_p[xm, yl, cc, :HALF]
                for d in (1, 2, 3):
                    value = value + decode(pa_in[d - 1, xm, cc], lane(sy1_in[d - 1]))
                fa_out[e, cc] = encode(value, inv_a)
            if e == 0:
                fa_in[0] = fa_out[0, c]
                sfa_in[0] = sc_pa[0]

        if e:
            back = 4 - e
            for cc in (0, 1):
                row(lambda cc=cc: (sc_pa.at[0], sfa_in.at[back], fas_sem.at[0], at_x(e, cc)), same)
                send(lambda cc=cc: (fa_out.at[e, cc], fa_in.at[back], fa_sem.at[0], at_x(e, cc)), same)
        else:
            row(lambda: (sc_pa.at[0], sfa_in.at[0], fas_sem.at[0], partner), same)
            send(lambda: (fa_out.at[0, other], fa_in.at[0], fa_sem.at[0], partner), same)

    relay_lower(2)
    relay_lower(1)
    relay_rows()
    relay_upper(0)
    relay_lower(3)
    relay_upper(1)
    relay_lower(0)

    value = column_sum(z)
    wait(halves_of(4), zd_sem.at[0])
    for i, d in ((0, 7), (1, 1)):
        value = value + decode(zd_in[i], lane(sz_in[d]))
    wait(rows_of(2), zsc2_sem.at[0])
    wait(halves_of(4), z2_sem.at[0])
    for i in (0, 1):
        value = value + decode(z2_in[i], lane(sz2_in[i]))
    oq_ref[...] = value

    for parts, scales, psem, sem, half in ((fb_in, sfb_in, fb_sem, fbs_sem, high), (fa_in, sfa_in, fa_sem, fas_sem, low)):
        for n, when in ((3, same), (4, apart)):

            @pl.when(when)
            def _(n=n, psem=psem, sem=sem):
                wait(rows_of(n), sem.at[0])
                wait(halves_of(n), psem.at[0])

        value = decode(parts[0], lane(scales[0]))
        for e in (1, 2, 3):
            value = value + decode(parts[e], lane(scales[e]))
        op_ref[half, :] = value

    settle()


N_SENDS = 22
Z_PEERS = (2, 6, 1, 7)
VMEM_LIMIT = 20 * 2**20


def local(queries, passages, query_lognorm, passage_lognorm, loss_cotangent):
    width = queries.shape[1]
    columns = passage_lognorm.shape[0]
    dma = pltpu.SemaphoreType.DMA
    vm = pltpu.VMEM
    scratch = [
        vm((16, ROWS, width), BF16), vm((16, ROWS, width), BF16), vm((ROWS, width), BF16), vm((16, 1, 128), F32), vm((1, columns), F32),
        vm((16 * ROWS, columns), BF16), vm((16 * ROWS, columns), BF16),
        vm((8, ROWS, width), F32), vm((4, 2, 2, ROWS, width), F32),
        vm((8, ROWS, width), F32), vm((8, ROWS, width), F32),
        vm((5, ROWS, width), BF16), vm((2, ROWS, width), BF16), vm((2, ROWS, width), BF16),
        vm((2, ROWS, width), BF16), vm((2, HALF, width), BF16), vm((2, ROWS, width), BF16),
        vm((2, 4, 2, HALF, width), BF16), vm((3, 4, 2, HALF, width), BF16),
        vm((3, 2, 2, HALF, width), BF16), vm((3, 2, 2, HALF, width), BF16),
        vm((4, 2, HALF, width), BF16), vm((4, HALF, width), BF16),
        vm((2, 2, HALF, width), BF16), vm((4, HALF, width), BF16),
        *[vm((n, 1, 128), F32) for n in (1, 1, 2, 1, 1, 1, 8, 2, 3, 3, 4, 4)],
        vm((8, HALF, width), BF16), pltpu.SMEM((ROWS,), F32), dma((N_SENDS,)), dma((7,)), dma((10,)), dma((8,)), dma((5,)), dma((3,)), dma((1,)),
        *[dma((n,)) for n in (1, 1, 1, 2, 1, 1, 1, 4, 2, 1, 1, 1, 1, 1, 1)],
    ]
    out = jax.ShapeDtypeStruct(queries.shape, F32)
    vmem = pl.BlockSpec(memory_space=pltpu.VMEM)

    def kernel(*refs):
        body(width, *refs)

    sums = pl.pallas_call(
        kernel,
        out_shape=(out, out),
        in_specs=[pl.BlockSpec(memory_space=pltpu.HBM)] * 4,
        out_specs=[vmem] * 2,
        scratch_shapes=scratch,
        compiler_params=pltpu.CompilerParams(collective_id=0, has_side_effects=True, vmem_limit_bytes=VMEM_LIMIT),
    )(*[pltpu.with_memory_space_constraint(v, pltpu.HBM) for v in (queries, passages, query_lognorm, passage_lognorm)])

    sums = lax.optimization_barrier((sums[0], sums[1], loss_cotangent))
    factor = sums[2] * (1.0 / math.sqrt(width))
    return sums[0] * factor, sums[1] * factor


def solution(mesh):
    return jax.shard_map(
        local,
        mesh=mesh,
        in_specs=(
            P(("slab", "blk"), None),
            P(("blk", "slab"), None),
            P(("slab", "blk")),
            P("blk"),
            P(),
        ),
        out_specs=(P(("slab", "blk"), None), P(("blk", "slab"), None)),
        check_vma=False,
    )
```
